256 devices in a mesh: frame: 32 (over y, z), coord: 8 (over x, core).
Axes of the slice: x: 4, y: 4, z: 8, core: 2. Of those that a mesh axis runs over, the one named last changes fastest.
Arguments:
- frames: bfloat16 [32768, 4224], P('frame'), may hold values from -0.5 to 1.5
- b_values: bfloat16 [4096, 512], P('coord'), may hold values from -0.25 to 0.25
- b_cols: int32 [64, 8], P('coord'), may hold values from 0 to 65, as said below
- frame_window: int32 [32768], P('frame'), may hold values from 0 to 1, as said below
Outputs:
- count: float32 [], replicated
- mean: float32 [4096], P('coord')
- covariance: float32 [4096, 4096], P('frame', 'coord')
The draws below stay inside these ranges and needn't reach their ends.
Inputs may be any that keep to these rules, and one draw needn't show every extreme that they name: `b_cols`: each row holds 8 different column-block indices. `frame_window`: the first and the last frame are always in the window.
All inputs are finite; a program needn't handle non-finite values.
Results may differ from the reference program's by a relative error of at most 0.0022.
Values may be sent and summed in bfloat16 or wider, within the bound.
A program may use at most 128 MiB of HBM per device.

```python
import jax
import jax.numpy as jnp
from jax import lax

CART = 4224
NQ = 4096
BLOCK = 64
KB = 8
FRAMES = 32768
CB = 66
NQB = 64


def draw_b_cols(key, part):
    row_keys = jax.random.split(key, NQB)
    chosen = jax.vmap(lambda row_key: jax.random.permutation(row_key, CB)[:KB])(row_keys)
    return chosen.astype(jnp.int32)


def draw_frame_window(key, part):
    index = jnp.arange(FRAMES, dtype=jnp.int32)
    rolls = jax.random.randint(key, (FRAMES,), 0, 4 * FRAMES, dtype=jnp.int32)
    inside = (rolls < FRAMES + 2 * index) | (index == 0) | (index == FRAMES - 1)
    return inside.astype(jnp.int32)


def steps_of(own_key, extent, pieces, low, top_value):
    factor_of = 1.0
    for dim, blocks in pieces:
        heights = jax.random.uniform(jax.random.fold_in(jax.random.fold_in(own_key, 6), dim), (blocks,), jnp.float32, low / len(pieces), top_value / len(pieces))
        factor_of = factor_of * jnp.repeat(jnp.exp(heights), extent[dim] // blocks).reshape((-1,) + (1,) * (len(extent) - 1 - dim))
    return factor_of


def noise(own_key, shape, scale, bound, shards=(), kind=jnp.bfloat16):
    drawn = scale * jax.random.normal(own_key, shape, jnp.float32)
    if shards:
        drawn = drawn * steps_of(own_key, shape, shards, -0.22, 0.18)
    return jnp.clip(drawn, -bound, bound).astype(kind)


def setup_inputs(seed: int = 0) -> dict:
    streams_of = jax.random.split(jax.random.key(seed), 5)
    frames = jnp.clip(-0.5 + 2.0 * jax.random.uniform(streams_of[0], (FRAMES, CART), jnp.float32) ** steps_of(streams_of[0], (FRAMES, CART), ((0, 32),), -0.2, 0.2), -0.5, 1.5).astype(jnp.bfloat16)
    b_values = noise(streams_of[1], (NQ, KB * BLOCK), (KB * BLOCK) ** -0.5, 0.25, ((0, 8),))
    b_cols = draw_b_cols(jax.random.fold_in(streams_of[4], 71), 0)
    frame_window = draw_frame_window(jax.random.fold_in(streams_of[4], 71), 0)
    return {"frames": frames, "b_values": b_values, "b_cols": b_cols, "frame_window": frame_window}


def reference(frames, b_values, b_cols, frame_window):
    blocks = frames.reshape(FRAMES, CB, BLOCK)

    def one_block(row_block):
        picked = jnp.take(blocks, b_cols[row_block], axis=1).reshape(FRAMES, KB * BLOCK)
        rows_here = lax.dynamic_slice_in_dim(b_values, (row_block * BLOCK).astype(jnp.int32), BLOCK, 0)
        product = lax.dot_general(picked, rows_here, (((1,), (1,)), ((), ())), preferred_element_type=jnp.float32)
        return product.astype(jnp.bfloat16)

    coords_q = lax.map(one_block, jnp.arange(NQB, dtype=jnp.int32))
    coords_q = jnp.transpose(coords_q, (1, 0, 2)).reshape(FRAMES, NQ)
    weight = frame_window.astype(jnp.float32)
    count = jnp.sum(weight)
    coords_f = coords_q.astype(jnp.float32)
    mean = jnp.dot(weight, coords_f, precision=lax.Precision.HIGHEST) / count
    centered = (weight[:, None] * (coords_f - mean)).astype(jnp.bfloat16)
    centered_f = centered.astype(jnp.float32)
    covariance = jnp.dot(centered_f.T, centered_f, precision=lax.Precision.HIGHEST) / (count - 1.0)
    return count, mean, covariance
```

```python
import functools

import jax
import jax.numpy as jnp
from jax import lax
from jax.experimental import pallas as pl
from jax.experimental.pallas import tpu as pltpu
from jax.sharding import PartitionSpec as P

BLOCK = 64
NY, NZ, NX = 4, 8, 4
NF, NC = NY * NZ, NX * 2
PANEL = 512
OWN = 128
MESH = pl.DeviceIdType.MESH
BF = jnp.bfloat16
F32 = jnp.float32


def densify(cols_ref, vals_ref, out_ref):
    out_ref[...] = jnp.zeros_like(out_ref)
    turned = vals_ref[...].T
    for r in range(8):
        lanes = slice(r * BLOCK, (r + 1) * BLOCK)
        for k in range(8):
            row = pl.multiple_of(cols_ref[r, k] * BLOCK, BLOCK)
            out_ref[pl.ds(row, BLOCK), lanes] = turned[k * BLOCK : (k + 1) * BLOCK, lanes]


def remote(src, dst, send_sem, recv_sem, device):
    return pltpu.make_async_remote_copy(
        src_ref=src, dst_ref=dst, send_sem=send_sem, recv_sem=recv_sem, device_id=device, device_id_type=MESH
    )


class Ring:
    def __init__(self, n, pos, peer, own, recv, send_sems, recv_sems, rows):
        self.n, self.pos, self.own, self.recv = n, pos, own, recv
        self.peer = [peer(lax.rem(pos + 1, n)), peer(lax.rem(pos + n - 1, n))]
        self.send_sems, self.recv_sems, self.rows = send_sems, recv_sems, rows
        self.half = [slice(rows // 2, rows), slice(0, rows // 2)]

    def target(self, d, s):
        steps = self.n // 2 - s
        return lax.rem(self.pos + (steps if d == 0 else self.n - steps), self.n)

    def copy(self, d, s):
        t = self.target(d, s)
        if s == 0:
            src = self.own.at[t, self.half[d]]
            dst = self.recv.at[d, 0, self.half[d]]
        else:
            src = self.recv.at[d, s - 1]
            dst = self.recv.at[d, s]
        return remote(src, dst, self.send_sems.at[d, s], self.recv_sems.at[d, s], self.peer[d])

    def start(self, d, s):
        if s > 0:
            self.copy(d, s - 1).wait_recv()
            t = self.target(d, s)
            buf = self.recv.at[d, s - 1]
            if s == 1:
                h, o = self.half[d], self.half[1 - d]
                buf[h] = (buf[h].astype(F32) + self.own[t, h].astype(F32)).astype(BF)
                buf[o] = self.own[t, o]
            else:
                buf[...] = (buf[...].astype(F32) + self.own[t].astype(F32)).astype(BF)
        self.copy(d, s).start()

    def finish(self):
        last = self.n // 2 - 1
        for d in range(2):
            self.copy(d, last).wait_recv()

    def total(self, sl=slice(None)):
        last = self.n // 2 - 1
        return (
            self.own[self.pos, sl].astype(F32) + self.recv[0, last, sl].astype(F32) + self.recv[1, last, sl].astype(F32)
        )

    def drain(self):
        for d in range(2):
            for s in range(self.n // 2):
                self.copy(d, s).wait_send()


def main_kernel(
    x_hbm, bdt_hbm, vals_ref, cols_ref, wrow_ref,
    count_ref, mean_ref, cov_ref,
    x, bdt, q, g, ball, cbuf, csm, sz, sy, xm, pa, pb, ra, rb, ay, az, bz, by,
    ld_sem, loc_sem, val_s, val_r, col_s, col_r, z_s, z_r, y_s, y_r,
    ay_s, ay_r, az_s, az_r, bz_s, bz_r, by_s, by_r,
):
    f, c = lax.axis_index("frame"), lax.axis_index("coord")
    yy, zz = f // NZ, lax.rem(f, NZ)
    xx, kk = c // 2, lax.rem(c, 2)
    rows_total = x.shape[0]
    XT = 4
    xr = rows_total // XT
    loads = [pltpu.make_async_copy(bdt_hbm, bdt, ld_sem.at[0])]
    for i in range(XT):
        sl = pl.ds(i * xr, xr)
        loads.append(pltpu.make_async_copy(x_hbm.at[sl], x.at[sl], ld_sem.at[i + 1]))
    for cp in loads:
        cp.start()

    def coord_peer(o):
        return (f, lax.rem(c + o, NC))

    def z_peer(o):
        return (yy * NZ + lax.rem(zz + o, NZ), c)

    def y_peer(o):
        return (lax.rem(yy + o, NY) * NZ + zz, c)

    x_up = (f, lax.rem(xx + 1, NX) * 2 + kk)
    x_dn = (f, lax.rem(xx + NX - 1, NX) * 2 + kk)
    sib = (f, xx * 2 + 1 - kk)

    barrier = pltpu.get_barrier_semaphore()
    peers = [coord_peer(o) for o in range(1, NC)] + [z_peer(o) for o in range(1, NZ)] + [y_peer(o) for o in range(1, NY)]
    for p in peers:
        pl.semaphore_signal(barrier, inc=1, device_id=p, device_id_type=MESH)
    pl.semaphore_wait(barrier, len(peers))

    c_up, c_dn, c_op = x_up[1], x_dn[1], lax.rem(c + 4, NC)
    lo, hi = pl.ds(0, 4), pl.ds(4, 4)
    own_vals = pltpu.make_async_copy(vals_ref, ball.at[c], loc_sem.at[0])
    own_cols = pltpu.make_async_copy(cols_ref, cbuf.at[c], loc_sem.at[1])
    own_vals.start()
    own_cols.start()
    v_up = remote(vals_ref, ball.at[c], val_s.at[0], val_r.at[0], x_up)
    v_dn = remote(vals_ref, ball.at[c], val_s.at[1], val_r.at[1], x_dn)
    v_sib = remote(vals_ref, ball.at[c], val_s.at[2], val_r.at[2], sib)
    for cp in (v_up, v_dn, v_sib):
        cp.start()
    col_copies = [
        remote(cols_ref, cbuf.at[c], col_s.at[o - 1], col_r.at[o - 1], coord_peer(o)) for o in range(1, NC)
    ]
    for cp in col_copies:
        cp.start()

    loads[0].wait()
    wrow = wrow_ref[...].astype(F32)
    sums = jnp.zeros((8, x.shape[1]), F32)
    for i in range(XT):
        loads[i + 1].wait()
        sl = slice(i * xr, (i + 1) * xr)
        q[sl] = jnp.dot(x[sl], bdt[...], preferred_element_type=F32).astype(BF)
        sums = sums + jnp.dot(wrow[:, sl].astype(BF), x[sl], preferred_element_type=F32)
    sums_q = jnp.dot(wrow.astype(BF), q[...], preferred_element_type=F32)
    cart = x.shape[1]
    sz[zz, :, :cart] = sums[0:1]
    sz[zz, :, cart : cart + PANEL] = sums_q[0:1]
    sz[zz, :, cart + PANEL :] = jnp.broadcast_to(jnp.sum(wrow[0:1], axis=1, keepdims=True), (1, 128))
    sz_copies = [remote(sz.at[zz], sz.at[zz], z_s.at[o - 1], z_r.at[o - 1], z_peer(o)) for o in range(1, NZ)]
    for cp in sz_copies:
        cp.start()

    v_up.wait_recv()
    f_up = remote(ball.at[c_dn, hi], ball.at[c_dn, hi], val_s.at[3], val_r.at[3], x_up)
    f_up.start()
    s_dn = remote(ball.at[c_dn], ball.at[c_dn], val_s.at[4], val_r.at[4], sib)
    s_dn.start()
    v_dn.wait_recv()
    f_dn = remote(ball.at[c_up, lo], ball.at[c_up, lo], val_s.at[5], val_r.at[5], x_dn)
    f_dn.start()
    s_up = remote(ball.at[c_up], ball.at[c_up], val_s.at[6], val_r.at[6], sib)
    s_up.start()

    for cp in sz_copies:
        cp.wait_recv()
    part = sz[0]
    for j in range(1, NZ):
        part = part + sz[j]
    sy[yy] = part
    sy_copies = [remote(sy.at[yy], sy.at[yy], y_s.at[o - 1], y_r.at[o - 1], y_peer(o)) for o in range(1, NY)]
    for cp in sy_copies:
        cp.start()
    wcol = jnp.broadcast_to(wrow[0:1], (128, rows_total)).T
    for cp in sy_copies:
        cp.wait_recv()
    whole = sy[0]
    for j in range(1, NY):
        whole = whole + sy[j]
    count_ref[...] = whole[:, cart + PANEL :]
    inverse = 1.0 / whole[:, cart + PANEL : cart + PANEL + 1]
    mean = whole[:, cart : cart + PANEL] / whole[:, cart + PANEL : cart + PANEL + 1]
    mean_ref[...] = mean
    xm[...] = whole[:, :cart] * inverse
    wide = jnp.concatenate([wcol] * (PANEL // 128), axis=1)
    q[...] = (wide * (q[...].astype(F32) - mean)).astype(BF)

    GT = 384

    def g_tile(i, carry):
        start = pl.multiple_of(i * GT, 128)
        moved = (x[:, pl.ds(start, GT)].astype(F32) - xm[:, pl.ds(start, GT)]).astype(BF)
        tile = lax.dot_general(
            moved, q[...], (((0,), (0,)), ((), ())), preferred_element_type=F32
        ).astype(BF)
        for b in range(GT // BLOCK):
            g[i * (GT // BLOCK) + b] = tile[b * BLOCK : (b + 1) * BLOCK]
        return carry

    lax.fori_loop(0, x.shape[1] // GT, g_tile, 0)

    f_up.wait_recv()
    f_dn.wait_recv()
    s_op = remote(ball.at[c_op], ball.at[c_op], val_s.at[7], val_r.at[7], sib)
    s_op.start()
    for cp in col_copies:
        cp.wait_recv()
    own_cols.wait()
    to_smem = pltpu.make_async_copy(cbuf, csm, loc_sem.at[1])
    to_smem.start()
    own_vals.wait()
    to_smem.wait()
    for cp in (v_sib, s_dn, s_up, s_op):
        cp.wait_recv()

    def p_tile(i, carry):
        yr, zr = i // NZ, lax.rem(i, NZ)
        for h in range(2):
            panel, row = i // 4, lax.rem(i, 4) * 2 + h
            picked = jnp.concatenate(
                [g[csm[panel, row, k]] for k in range(8)], axis=0
            )
            out = jnp.dot(ball[panel, row], picked, preferred_element_type=F32).astype(BF)
            pa[yr, zr, h * BLOCK : (h + 1) * BLOCK] = out[:, : PANEL // 2]
            pb[zr, yr, h * BLOCK : (h + 1) * BLOCK] = out[:, PANEL // 2 :]
        return carry

    lax.fori_loop(0, NF, p_tile, 0)

    ring_ay = Ring(NY, yy, lambda t: (t * NZ + zz, c), pa, ay, ay_s, ay_r, NZ)
    ring_bz = Ring(NZ, zz, lambda t: (yy * NZ + t, c), pb, bz, bz_s, bz_r, NY)
    for d in range(2):
        ring_ay.start(d, 0)
        ring_bz.start(d, 0)
    for d in range(2):
        ring_bz.start(d, 1)
    for d in range(2):
        ring_ay.start(d, 1)
    for s in (2, 3):
        for d in range(2):
            ring_bz.start(d, s)
    ring_ay.finish()
    ra[...] = ring_ay.total().astype(BF)
    az_copies = [
        remote(ra.at[lax.rem(zz + o, NZ)], az.at[o - 1], az_s.at[o - 1], az_r.at[o - 1], z_peer(o)) for o in range(1, NZ)
    ]
    for cp in az_copies:
        cp.start()
    ring_bz.finish()
    rb[...] = ring_bz.total().astype(BF)
    by_copies = [
        remote(rb.at[lax.rem(yy + o, NY)], by.at[o - 1], by_s.at[o - 1], by_r.at[o - 1], y_peer(o)) for o in range(1, NY)
    ]
    for cp in by_copies:
        cp.start()
    scale = 1.0 / (whole[:, cart + PANEL : cart + PANEL + 1] - 1.0)
    total = ra[zz].astype(F32)
    for o in range(1, NZ):
        az_copies[o - 1].wait_recv()
        total = total + az[o - 1].astype(F32)
    cov_ref[:, : PANEL // 2] = total * scale
    total = rb[yy].astype(F32)
    for o in range(1, NY):
        by_copies[o - 1].wait_recv()
        total = total + by[o - 1].astype(F32)
    cov_ref[:, PANEL // 2 :] = total * scale

    for ring in (ring_ay, ring_bz):
        ring.drain()
    for cp in (v_up, v_dn, v_sib, f_up, f_dn, s_dn, s_up, s_op, *col_copies, *sz_copies, *sy_copies, *az_copies, *by_copies):
        cp.wait_send()


def on_device(frames, b_values, b_cols, frame_window):
    rows, cart = frames.shape
    vmem = pl.BlockSpec(memory_space=pltpu.VMEM)
    hbm = pl.BlockSpec(memory_space=pl.ANY)
    bdt = pl.pallas_call(
        densify,
        out_shape=jax.ShapeDtypeStruct((cart, PANEL), BF),
        in_specs=[pl.BlockSpec(memory_space=pltpu.SMEM), vmem],
        out_specs=vmem,
        name="densify",
    )(b_cols, b_values)
    cols = jnp.pad(b_cols, ((0, 0), (0, 120)))
    wrow = jnp.broadcast_to(frame_window.reshape(1, rows), (8, rows))
    dma = pltpu.SemaphoreType.DMA
    count, mean, cov = pl.pallas_call(
        main_kernel,
        out_shape=(
            jax.ShapeDtypeStruct((1, 128), F32),
            jax.ShapeDtypeStruct((1, PANEL), F32),
            jax.ShapeDtypeStruct((OWN, PANEL), F32),
        ),
        in_specs=[hbm, hbm, vmem, vmem, vmem],
        out_specs=(vmem, vmem, vmem),
        scratch_shapes=[
            pltpu.VMEM((rows, cart), BF),
            pltpu.VMEM((cart, PANEL), BF),
            pltpu.VMEM((rows, PANEL), BF),
            pltpu.VMEM((cart // BLOCK, BLOCK, PANEL), BF),
            pltpu.VMEM((NC, 8, BLOCK, PANEL), BF),
            pltpu.VMEM((NC, 8, 128), jnp.int32),
            pltpu.SMEM((NC, 8, 128), jnp.int32),
            pltpu.VMEM((NZ, 1, cart + PANEL + 128), F32),
            pltpu.VMEM((NY, 1, cart + PANEL + 128), F32),
            pltpu.VMEM((1, cart), F32),
            pltpu.VMEM((NY, NZ, OWN, PANEL // 2), BF),
            pltpu.VMEM((NZ, NY, OWN, PANEL // 2), BF),
            pltpu.VMEM((NZ, OWN, PANEL // 2), BF),
            pltpu.VMEM((NY, OWN, PANEL // 2), BF),
            pltpu.VMEM((2, NY // 2, NZ, OWN, PANEL // 2), BF),
            pltpu.VMEM((NZ - 1, OWN, PANEL // 2), BF),
            pltpu.VMEM((2, NZ // 2, NY, OWN, PANEL // 2), BF),
            pltpu.VMEM((NY - 1, OWN, PANEL // 2), BF),
            dma((5,)), dma((2,)), dma((8,)), dma((8,)), dma((7,)), dma((7,)),
            dma((NZ - 1,)), dma((NZ - 1,)), dma((NY - 1,)), dma((NY - 1,)),
            dma((2, NY // 2)), dma((2, NY // 2)), dma((NZ - 1,)), dma((NZ - 1,)),
            dma((2, NZ // 2)), dma((2, NZ // 2)), dma((NY - 1,)), dma((NY - 1,)),
        ],
        compiler_params=pltpu.CompilerParams(
            collective_id=0, has_side_effects=True, vmem_limit_bytes=60 * 1024 * 1024
        ),
        name="covariance",
    )(frames, bdt, b_values.reshape(8, BLOCK, PANEL), cols, wrow)
    return count[0, 0], mean.reshape(PANEL), cov


def solution(mesh):
    return jax.shard_map(
        on_device,
        mesh=mesh,
        in_specs=(P("frame", None), P("coord", None), P("coord", None), P("frame")),
        out_specs=(P(), P("coord"), P("frame", "coord")),
        check_vma=False,
    )
```

```python
import functools

import jax
import jax.numpy as jnp
from jax import lax
from jax.experimental import pallas as pl
from jax.experimental.pallas import tpu as pltpu
from jax.sharding import PartitionSpec as P

BLOCK = 64
NY, NZ, NX = 4, 8, 4
NF, NC = NY * NZ, NX * 2
PANEL = 512
OWN = 128
LANES = 128
NA = 3
MESH = pl.DeviceIdType.MESH
BF = jnp.bfloat16
F32 = jnp.float32


def densify(cols_ref, cols_vec_ref, vals_ref, out_ref, wide_cols_ref):
    out_ref[...] = jnp.zeros_like(out_ref)
    wide_cols_ref[:, 0:8] = cols_vec_ref[...]
    wide_cols_ref[:, 8:] = jnp.zeros((8, 120), jnp.int32)
    turned = vals_ref[...].T
    for r in range(8):
        lanes = slice(r * BLOCK, (r + 1) * BLOCK)
        for k in range(8):
            row = pl.multiple_of(cols_ref[r, k] * BLOCK, BLOCK)
            out_ref[pl.ds(row, BLOCK), lanes] = turned[k * BLOCK : (k + 1) * BLOCK, lanes]


def remote(src, dst, send_sem, recv_sem, device):
    return pltpu.make_async_remote_copy(
        src_ref=src, dst_ref=dst, send_sem=send_sem, recv_sem=recv_sem, device_id=device, device_id_type=MESH
    )


class Ring:
    def __init__(self, n, pos, peer, own, recv, send_sems, recv_sems, rows):
        self.n, self.pos, self.own, self.recv = n, pos, own, recv
        self.peer = [peer(lax.rem(pos + 1, n)), peer(lax.rem(pos + n - 1, n))]
        self.send_sems, self.recv_sems, self.rows = send_sems, recv_sems, rows
        self.half = [slice(rows // 2, rows), slice(0, rows // 2)]

    def target(self, d, s):
        steps = self.n // 2 - s
        return lax.rem(self.pos + (steps if d == 0 else self.n - steps), self.n)

    def copy(self, d, s):
        t = self.target(d, s)
        if s == 0:
            src = self.own.at[t, self.half[d]]
            dst = self.recv.at[d, 0, self.half[d]]
        else:
            src = self.recv.at[d, s - 1]
            dst = self.recv.at[d, s]
        return remote(src, dst, self.send_sems.at[d, s], self.recv_sems.at[d, s], self.peer[d])

    def start(self, d, s):
        if s > 0:
            self.copy(d, s - 1).wait_recv()
            t = self.target(d, s)
            buf = self.recv.at[d, s - 1]
            if s == 1:
                h, o = self.half[d], self.half[1 - d]
                buf[h] = (buf[h].astype(F32) + self.own[t, h].astype(F32)).astype(BF)
                buf[o] = self.own[t, o]
            else:
                buf[...] = (buf[...].astype(F32) + self.own[t].astype(F32)).astype(BF)
        self.copy(d, s).start()

    def finish(self):
        last = self.n // 2 - 1
        for d in range(2):
            self.copy(d, last).wait_recv()

    def total(self, sl=slice(None)):
        last = self.n // 2 - 1
        return (
            self.own[self.pos, sl].astype(F32) + self.recv[0, last, sl].astype(F32) + self.recv[1, last, sl].astype(F32)
        )

    def drain(self):
        for d in range(2):
            for s in range(self.n // 2):
                self.copy(d, s).wait_send()


def main_kernel(
    x_hbm, bdt_hbm, vals_ref, cols_ref, wrow_ref,
    count_ref, mean_ref, cov_ref,
    x, bdt, q, g, ball, cbuf, csm, xz, xy, sz, sy, xm, pa, pb, ra, rb, ay, az, bz, by,
    ld_sem, loc_sem, val_s, val_r, col_s, col_r, xz_s, xz_r, xy_s, xy_r, z_s, z_r, y_s, y_r,
    ay_s, ay_r, az_s, az_r, bz_s, bz_r, by_s, by_r,
):
    f, c = lax.axis_index("frame"), lax.axis_index("coord")
    yy, zz = f // NZ, lax.rem(f, NZ)
    xx, kk = c // 2, lax.rem(c, 2)
    rows_total = x.shape[0]
    XT = 4
    xr = rows_total // XT
    loads = [pltpu.make_async_copy(bdt_hbm, bdt, ld_sem.at[0])]
    for i in range(XT):
        sl = pl.ds(i * xr, xr)
        loads.append(pltpu.make_async_copy(x_hbm.at[sl], x.at[sl], ld_sem.at[i + 1]))
    for cp in loads:
        cp.start()

    def coord_peer(o):
        return (f, lax.rem(c + o, NC))

    def z_peer(o):
        return (yy * NZ + lax.rem(zz + o, NZ), c)

    def y_peer(o):
        return (lax.rem(yy + o, NY) * NZ + zz, c)

    x_up = (f, lax.rem(xx + 1, NX) * 2 + kk)
    x_dn = (f, lax.rem(xx + NX - 1, NX) * 2 + kk)
    sib = (f, xx * 2 + 1 - kk)

    barrier = pltpu.get_barrier_semaphore()
    peers = [coord_peer(o) for o in range(1, NC)] + [z_peer(o) for o in range(1, NZ)] + [y_peer(o) for o in range(1, NY)]
    for p in peers:
        pl.semaphore_signal(barrier, inc=1, device_id=p, device_id_type=MESH)
    pl.semaphore_wait(barrier, len(peers))

    c_up, c_dn, c_op = x_up[1], x_dn[1], lax.rem(c + 4, NC)
    lo, hi = pl.ds(0, 4), pl.ds(4, 4)
    own_vals = pltpu.make_async_copy(vals_ref, ball.at[c], loc_sem.at[0])
    own_cols = pltpu.make_async_copy(cols_ref, cbuf.at[c], loc_sem.at[1])
    own_vals.start()
    own_cols.start()
    v_up = remote(vals_ref, ball.at[c], val_s.at[0], val_r.at[0], x_up)
    v_dn = remote(vals_ref, ball.at[c], val_s.at[1], val_r.at[1], x_dn)
    v_sib = remote(vals_ref, ball.at[c], val_s.at[2], val_r.at[2], sib)
    for cp in (v_up, v_dn, v_sib):
        cp.start()
    col_copies = [
        remote(cols_ref, cbuf.at[c], col_s.at[o - 1], col_r.at[o - 1], coord_peer(o)) for o in range(1, NC)
    ]
    for cp in col_copies:
        cp.start()

    loads[0].wait()
    wrow = jnp.broadcast_to(wrow_ref[...].astype(F32), (8, rows_total))
    whalf = wrow.astype(BF)
    sums = jnp.zeros((8, x.shape[1]), F32)

    def project(i):
        sl = slice(i * xr, (i + 1) * xr)
        q[sl] = jnp.dot(x[sl], bdt[...], preferred_element_type=F32).astype(BF)

    for i in range(XT):
        loads[i + 1].wait()
        sl = slice(i * xr, (i + 1) * xr)
        sums = sums + jnp.dot(whalf[:, sl], x[sl], preferred_element_type=F32)
        if i < XT - 1:
            project(i)

    def all_to_all(buf, mine, peer, n, send_sems, recv_sems):
        copies = [remote(buf.at[mine], buf.at[mine], send_sems.at[o - 1], recv_sems.at[o - 1], peer(o)) for o in range(1, n)]
        for cp in copies:
            cp.start()
        return copies

    def gathered(buf, copies):
        for cp in copies:
            cp.wait_recv()
        part = buf[0]
        for j in range(1, buf.shape[0]):
            part = part + buf[j]
        return part

    xz[zz] = sums[0:1]
    xz_copies = all_to_all(xz, zz, z_peer, NZ, xz_s, xz_r)
    project(XT - 1)
    sz[zz, :, :PANEL] = jnp.dot(whalf, q[...], preferred_element_type=F32)[0:1]
    sz[zz, :, PANEL:] = jnp.broadcast_to(jnp.sum(wrow[0:1], axis=1, keepdims=True), (1, 128))
    sz_copies = all_to_all(sz, zz, z_peer, NZ, z_s, z_r)

    v_up.wait_recv()
    f_up = remote(ball.at[c_dn, hi], ball.at[c_dn, hi], val_s.at[3], val_r.at[3], x_up)
    f_up.start()
    s_dn = remote(ball.at[c_dn], ball.at[c_dn], val_s.at[4], val_r.at[4], sib)
    s_dn.start()
    v_dn.wait_recv()
    f_dn = remote(ball.at[c_up, lo], ball.at[c_up, lo], val_s.at[5], val_r.at[5], x_dn)
    f_dn.start()
    s_up = remote(ball.at[c_up], ball.at[c_up], val_s.at[6], val_r.at[6], sib)
    s_up.start()

    xy[yy] = gathered(xz, xz_copies)
    xy_copies = all_to_all(xy, yy, y_peer, NY, xy_s, xy_r)
    sy[yy] = gathered(sz, sz_copies)
    sy_copies = all_to_all(sy, yy, y_peer, NY, y_s, y_r)
    wcol = jnp.broadcast_to(wrow[0:1], (128, rows_total)).T
    whole_x = gathered(xy, xy_copies)
    whole = gathered(sy, sy_copies)
    count_ref[...] = whole[:, PANEL:]
    count = whole[:, PANEL : PANEL + 1]
    mean = whole[:, :PANEL] / count
    mean_ref[...] = mean
    xm[...] = whole_x * (1.0 / count)
    wide = jnp.concatenate([wcol] * (PANEL // 128), axis=1)
    q[...] = (wide * (q[...].astype(F32) - mean)).astype(BF)

    GT = 384

    def g_tile(i, carry):
        start = pl.multiple_of(i * GT, 128)
        moved = (x[:, pl.ds(start, GT)].astype(F32) - xm[:, pl.ds(start, GT)]).astype(BF)
        tile = lax.dot_general(
            moved, q[...], (((0,), (0,)), ((), ())), preferred_element_type=F32
        ).astype(BF)
        for b in range(GT // BLOCK):
            g[i * (GT // BLOCK) + b] = tile[b * BLOCK : (b + 1) * BLOCK]
        return carry

    lax.fori_loop(0, x.shape[1] // GT, g_tile, 0)

    f_up.wait_recv()
    f_dn.wait_recv()
    s_op = remote(ball.at[c_op], ball.at[c_op], val_s.at[7], val_r.at[7], sib)
    s_op.start()
    for cp in col_copies:
        cp.wait_recv()
    own_cols.wait()
    to_smem = pltpu.make_async_copy(cbuf, csm, loc_sem.at[1])
    to_smem.start()
    own_vals.wait()
    to_smem.wait()
    for cp in (v_sib, s_dn, s_up, s_op):
        cp.wait_recv()

    def p_tile(yr, zr):
        panel = yr * 2 + zr // 4
        for h in range(2):
            row = lax.rem(zr, 4) * 2 + h
            picked = jnp.concatenate([g[csm[panel, row, k]] for k in range(8)], axis=0)
            out = jnp.dot(ball[panel, row], picked, preferred_element_type=F32).astype(BF)
            sl = slice(h * BLOCK, (h + 1) * BLOCK)
            for a in range(NA):
                pa[a, yr, zr, sl] = out[:, a * LANES : (a + 1) * LANES]
            pb[zr, yr, sl] = out[:, NA * LANES :]

    def tiles(n, where):
        def step(i, carry):
            p_tile(*where(i))
            return carry

        lax.fori_loop(0, n, step, 0)

    def y_at(o):
        return lax.rem(yy + o, NY)

    def z_at(o):
        return lax.rem(zz + o, NZ)

    ring_a = [
        Ring(NY, yy, lambda t: (t * NZ + zz, c), pa.at[a], ay.at[a], ay_s.at[a], ay_r.at[a], NZ) for a in range(NA)
    ]
    ring_b = Ring(NZ, zz, lambda t: (yy * NZ + t, c), pb, bz, bz_s, bz_r, NY)

    def both(ring, s):
        for d in range(2):
            ring.start(d, s)

    tiles(NZ, lambda i: (y_at(2), i))
    for a in range(NA):
        both(ring_a[a], 0)
    tiles(NY - 1, lambda i: (y_at(i + 3), z_at(4)))
    both(ring_b, 0)
    tiles(NZ - 1, lambda i: (y_at(1), z_at(i + 5)))
    tiles(NZ - 1, lambda i: (y_at(3), z_at(i + 5)))
    both(ring_a[0], 1)
    tiles(NZ - 1, lambda i: (yy, z_at(i + 5)))
    both(ring_b, 1)
    both(ring_a[1], 1)
    both(ring_b, 2)
    both(ring_a[2], 1)
    both(ring_b, 3)

    az_copies, by_copies = [], []

    def second(a):
        ring_a[a].finish()
        ra[a] = ring_a[a].total().astype(BF)
        az_copies.append(
            [remote(ra.at[a, z_at(o)], az.at[a, o - 1], az_s.at[a, o - 1], az_r.at[a, o - 1], z_peer(o)) for o in range(1, NZ)]
        )
        for cp in az_copies[a]:
            cp.start()

    second(0)
    ring_b.finish()
    rb[...] = ring_b.total().astype(BF)
    for o in range(1, NY):
        by_copies.append(remote(rb.at[y_at(o)], by.at[o - 1], by_s.at[o - 1], by_r.at[o - 1], y_peer(o)))
    for cp in by_copies:
        cp.start()
    for a in range(1, NA):
        second(a)
    scale = 1.0 / (count - 1.0)
    total = rb[yy].astype(F32)
    for o in range(1, NY):
        by_copies[o - 1].wait_recv()
        total = total + by[o - 1].astype(F32)
    cov_ref[:, NA * LANES :] = total * scale
    for a in range(NA):
        total = ra[a, zz].astype(F32)
        for o in range(1, NZ):
            az_copies[a][o - 1].wait_recv()
            total = total + az[a, o - 1].astype(F32)
        cov_ref[:, a * LANES : (a + 1) * LANES] = total * scale

    for ring in (*ring_a, ring_b):
        ring.drain()
    for copies in (*az_copies, by_copies, xz_copies, xy_copies, sz_copies, sy_copies, col_copies):
        for cp in copies:
            cp.wait_send()
    for cp in (v_up, v_dn, v_sib, f_up, f_dn, s_dn, s_up, s_op):
        cp.wait_send()


def on_device(frames, b_values, b_cols, frame_window):
    rows, cart = frames.shape
    vmem = pl.BlockSpec(memory_space=pltpu.VMEM)
    hbm = pl.BlockSpec(memory_space=pl.ANY)
    bdt, cols = pl.pallas_call(
        densify,
        out_shape=(jax.ShapeDtypeStruct((cart, PANEL), BF), jax.ShapeDtypeStruct((8, 128), jnp.int32)),
        in_specs=[pl.BlockSpec(memory_space=pltpu.SMEM), vmem, vmem],
        out_specs=(vmem, vmem),
        name="densify",
    )(b_cols, b_cols, b_values)
    wrow = frame_window.reshape(1, rows)
    dma = pltpu.SemaphoreType.DMA
    count, mean, cov = pl.pallas_call(
        main_kernel,
        out_shape=(
            jax.ShapeDtypeStruct((1, 128), F32),
            jax.ShapeDtypeStruct((1, PANEL), F32),
            jax.ShapeDtypeStruct((OWN, PANEL), F32),
        ),
        in_specs=[hbm, hbm, vmem, vmem, vmem],
        out_specs=(vmem, vmem, vmem),
        scratch_shapes=[
            pltpu.VMEM((rows, cart), BF),
            pltpu.VMEM((cart, PANEL), BF),
            pltpu.VMEM((rows, PANEL), BF),
            pltpu.VMEM((cart // BLOCK, BLOCK, PANEL), BF),
            pltpu.VMEM((NC, 8, BLOCK, PANEL), BF),
            pltpu.VMEM((NC, 8, 128), jnp.int32),
            pltpu.SMEM((NC, 8, 128), jnp.int32),
            pltpu.VMEM((NZ, 1, cart), F32),
            pltpu.VMEM((NY, 1, cart), F32),
            pltpu.VMEM((NZ, 1, PANEL + 128), F32),
            pltpu.VMEM((NY, 1, PANEL + 128), F32),
            pltpu.VMEM((1, cart), F32),
            pltpu.VMEM((NA, NY, NZ, OWN, LANES), BF),
            pltpu.VMEM((NZ, NY, OWN, LANES), BF),
            pltpu.VMEM((NA, NZ, OWN, LANES), BF),
            pltpu.VMEM((NY, OWN, LANES), BF),
            pltpu.VMEM((NA, 2, NY // 2, NZ, OWN, LANES), BF),
            pltpu.VMEM((NA, NZ - 1, OWN, LANES), BF),
            pltpu.VMEM((2, NZ // 2, NY, OWN, LANES), BF),
            pltpu.VMEM((NY - 1, OWN, LANES), BF),
            dma((5,)), dma((2,)), dma((8,)), dma((8,)), dma((7,)), dma((7,)),
            dma((NZ - 1,)), dma((NZ - 1,)), dma((NY - 1,)), dma((NY - 1,)),
            dma((NZ - 1,)), dma((NZ - 1,)), dma((NY - 1,)), dma((NY - 1,)),
            dma((NA, 2, NY // 2)), dma((NA, 2, NY // 2)), dma((NA, NZ - 1)), dma((NA, NZ - 1)),
            dma((2, NZ // 2)), dma((2, NZ // 2)), dma((NY - 1,)), dma((NY - 1,)),
        ],
        compiler_params=pltpu.CompilerParams(
            collective_id=0, has_side_effects=True, vmem_limit_bytes=60 * 1024 * 1024
        ),
        name="covariance",
    )(frames, bdt, b_values.reshape(8, BLOCK, PANEL), cols, wrow)
    return count[0, 0], mean.reshape(PANEL), cov


def solution(mesh):
    return jax.shard_map(
        on_device,
        mesh=mesh,
        in_specs=(P("frame", None), P("coord", None), P("coord", None), P("frame")),
        out_specs=(P(), P("coord"), P("frame", "coord")),
        check_vma=False,
    )
```

```python
import functools

import jax
import jax.numpy as jnp
from jax import lax
from jax.experimental import pallas as pl
from jax.experimental.pallas import tpu as pltpu
from jax.sharding import PartitionSpec as P

BLOCK = 64
NY, NZ, NX = 4, 8, 4
NF, NC = NY * NZ, NX * 2
PANEL = 512
OWN = 128
LANES = 128
NA = 3
MESH = pl.DeviceIdType.MESH
BF = jnp.bfloat16
F32 = jnp.float32


def densify(cols_ref, cols_vec_ref, vals_ref, out_ref, wide_cols_ref):
    out_ref[...] = jnp.zeros_like(out_ref)
    wide_cols_ref[:, 0:8] = cols_vec_ref[...]
    wide_cols_ref[:, 8:] = jnp.zeros((8, 120), jnp.int32)
    turned = vals_ref[...].T
    for r in range(8):
        lanes = slice(r * BLOCK, (r + 1) * BLOCK)
        for k in range(8):
            row = pl.multiple_of(cols_ref[r, k] * BLOCK, BLOCK)
            out_ref[pl.ds(row, BLOCK), lanes] = turned[k * BLOCK : (k + 1) * BLOCK, lanes]


def remote(src, dst, send_sem, recv_sem, device):
    return pltpu.make_async_remote_copy(
        src_ref=src, dst_ref=dst, send_sem=send_sem, recv_sem=recv_sem, device_id=device, device_id_type=MESH
    )


class Ring:
    def __init__(self, n, pos, peer, own, recv, send_sems, recv_sems, rows):
        self.n, self.pos, self.own, self.recv = n, pos, own, recv
        self.peer = [peer(lax.rem(pos + 1, n)), peer(lax.rem(pos + n - 1, n))]
        self.send_sems, self.recv_sems, self.rows = send_sems, recv_sems, rows
        self.half = [slice(rows // 2, rows), slice(0, rows // 2)]

    def target(self, d, s):
        steps = self.n // 2 - s
        return lax.rem(self.pos + (steps if d == 0 else self.n - steps), self.n)

    def copy(self, d, s):
        t = self.target(d, s)
        if s == 0:
            src = self.own.at[t, self.half[d]]
            dst = self.recv.at[d, 0, self.half[d]]
        else:
            src = self.recv.at[d, s - 1]
            dst = self.recv.at[d, s]
        return remote(src, dst, self.send_sems.at[d, s], self.recv_sems.at[d, s], self.peer[d])

    def start(self, d, s):
        if s > 0:
            self.copy(d, s - 1).wait_recv()
            t = self.target(d, s)
            buf = self.recv.at[d, s - 1]
            if s == 1:
                h, o = self.half[d], self.half[1 - d]
                buf[h] = (buf[h].astype(F32) + self.own[t, h].astype(F32)).astype(BF)
                buf[o] = self.own[t, o]
            else:
                buf[...] = (buf[...].astype(F32) + self.own[t].astype(F32)).astype(BF)
        self.copy(d, s).start()

    def finish(self):
        last = self.n // 2 - 1
        for d in range(2):
            self.copy(d, last).wait_recv()

    def total(self, sl=slice(None)):
        last = self.n // 2 - 1
        return (
            self.own[self.pos, sl].astype(F32) + self.recv[0, last, sl].astype(F32) + self.recv[1, last, sl].astype(F32)
        )

    def drain(self):
        for d in range(2):
            for s in range(self.n // 2):
                self.copy(d, s).wait_send()


def main_kernel(
    x_hbm, bdt_hbm, vals_ref, cols_ref, wrow_ref,
    count_ref, mean_ref, cov_ref,
    x, bdt, q, g, ball, cbuf, csm, xz, xy, sz, sy, xm, pa, pb, ra, rb, ay, az, bz, by,
    ld_sem, loc_sem, val_s, val_r, col_s, col_r, xz_s, xz_r, xy_s, xy_r, z_s, z_r, y_s, y_r,
    ay_s, ay_r, az_s, az_r, bz_s, bz_r, by_s, by_r,
):
    f, c = lax.axis_index("frame"), lax.axis_index("coord")
    yy, zz = f // NZ, lax.rem(f, NZ)
    xx, kk = c // 2, lax.rem(c, 2)
    rows_total = x.shape[0]
    XT = 4
    xr = rows_total // XT
    loads = [pltpu.make_async_copy(bdt_hbm, bdt, ld_sem.at[0])]
    for i in range(XT):
        sl = pl.ds(i * xr, xr)
        loads.append(pltpu.make_async_copy(x_hbm.at[sl], x.at[sl], ld_sem.at[i + 1]))
    for cp in loads:
        cp.start()

    def coord_peer(o):
        return (f, lax.rem(c + o, NC))

    def z_peer(o):
        return (yy * NZ + lax.rem(zz + o, NZ), c)

    def y_peer(o):
        return (lax.rem(yy + o, NY) * NZ + zz, c)

    x_up = (f, lax.rem(xx + 1, NX) * 2 + kk)
    x_dn = (f, lax.rem(xx + NX - 1, NX) * 2 + kk)
    sib = (f, xx * 2 + 1 - kk)

    barrier = pltpu.get_barrier_semaphore()
    peers = [coord_peer(o) for o in range(1, NC)] + [z_peer(o) for o in range(1, NZ)] + [y_peer(o) for o in range(1, NY)]
    for p in peers:
        pl.semaphore_signal(barrier, inc=1, device_id=p, device_id_type=MESH)
    pl.semaphore_wait(barrier, len(peers))

    c_up, c_dn, c_op = x_up[1], x_dn[1], lax.rem(c + 4, NC)
    lo, hi = pl.ds(0, 4), pl.ds(4, 4)
    own_vals = pltpu.make_async_copy(vals_ref, ball.at[c], loc_sem.at[0])
    own_cols = pltpu.make_async_copy(cols_ref, cbuf.at[c], loc_sem.at[1])
    own_vals.start()
    own_cols.start()
    v_up = remote(vals_ref, ball.at[c], val_s.at[0], val_r.at[0], x_up)
    v_dn = remote(vals_ref, ball.at[c], val_s.at[1], val_r.at[1], x_dn)
    v_sib = remote(vals_ref, ball.at[c], val_s.at[2], val_r.at[2], sib)
    for cp in (v_up, v_dn, v_sib):
        cp.start()
    col_copies = [
        remote(cols_ref, cbuf.at[c], col_s.at[o - 1], col_r.at[o - 1], coord_peer(o)) for o in range(1, NC)
    ]
    for cp in col_copies:
        cp.start()

    loads[0].wait()
    wrow = jnp.broadcast_to(wrow_ref[...].astype(F32), (8, rows_total))
    whalf = wrow.astype(BF)
    sums = jnp.zeros((8, x.shape[1]), F32)

    def project(i):
        sl = slice(i * xr, (i + 1) * xr)
        q[sl] = jnp.dot(x[sl], bdt[...], preferred_element_type=F32).astype(BF)

    for i in range(XT):
        loads[i + 1].wait()
        sl = slice(i * xr, (i + 1) * xr)
        sums = sums + jnp.dot(whalf[:, sl], x[sl], preferred_element_type=F32)
        if i < XT - 1:
            project(i)

    def all_to_all(buf, mine, peer, n, send_sems, recv_sems):
        copies = [remote(buf.at[mine], buf.at[mine], send_sems.at[o - 1], recv_sems.at[o - 1], peer(o)) for o in range(1, n)]
        for cp in copies:
            cp.start()
        return copies

    def gathered(buf, copies):
        for cp in copies:
            cp.wait_recv()
        part = buf[0]
        for j in range(1, buf.shape[0]):
            part = part + buf[j]
        return part

    xz[zz] = sums[0:1]
    xz_copies = all_to_all(xz, zz, z_peer, NZ, xz_s, xz_r)
    project(XT - 1)
    sz[zz, :, :PANEL] = jnp.dot(whalf, q[...], preferred_element_type=F32)[0:1]
    sz[zz, :, PANEL:] = jnp.broadcast_to(jnp.sum(wrow[0:1], axis=1, keepdims=True), (1, 128))
    sz_copies = all_to_all(sz, zz, z_peer, NZ, z_s, z_r)

    xy[yy] = gathered(xz, xz_copies)
    xy_copies = all_to_all(xy, yy, y_peer, NY, xy_s, xy_r)
    sy[yy] = gathered(sz, sz_copies)
    sy_copies = all_to_all(sy, yy, y_peer, NY, y_s, y_r)
    v_up.wait_recv()
    f_up = remote(ball.at[c_dn, hi], ball.at[c_dn, hi], val_s.at[3], val_r.at[3], x_up)
    f_up.start()
    s_dn = remote(ball.at[c_dn], ball.at[c_dn], val_s.at[4], val_r.at[4], sib)
    s_dn.start()
    v_dn.wait_recv()
    f_dn = remote(ball.at[c_up, lo], ball.at[c_up, lo], val_s.at[5], val_r.at[5], x_dn)
    f_dn.start()
    s_up = remote(ball.at[c_up], ball.at[c_up], val_s.at[6], val_r.at[6], sib)
    s_up.start()

    wcol = jnp.broadcast_to(wrow[0:1], (128, rows_total)).T
    whole_x = gathered(xy, xy_copies)
    whole = gathered(sy, sy_copies)
    count_ref[...] = whole[:, PANEL:]
    count = whole[:, PANEL : PANEL + 1]
    mean = whole[:, :PANEL] / count
    mean_ref[...] = mean
    xm[...] = whole_x * (1.0 / count)
    wide = jnp.concatenate([wcol] * (PANEL // 128), axis=1)
    q[...] = (wide * (q[...].astype(F32) - mean)).astype(BF)

    GT = 384

    def g_tile(i, carry):
        start = pl.multiple_of(i * GT, 128)
        moved = (x[:, pl.ds(start, GT)].astype(F32) - xm[:, pl.ds(start, GT)]).astype(BF)
        tile = lax.dot_general(
            moved, q[...], (((0,), (0,)), ((), ())), preferred_element_type=F32
        ).astype(BF)
        for b in range(GT // BLOCK):
            g[i * (GT // BLOCK) + b] = tile[b * BLOCK : (b + 1) * BLOCK]
        return carry

    lax.fori_loop(0, x.shape[1] // GT, g_tile, 0)

    f_up.wait_recv()
    f_dn.wait_recv()
    s_op = remote(ball.at[c_op], ball.at[c_op], val_s.at[7], val_r.at[7], sib)
    s_op.start()
    for cp in col_copies:
        cp.wait_recv()
    own_cols.wait()
    to_smem = pltpu.make_async_copy(cbuf, csm, loc_sem.at[1])
    to_smem.start()
    own_vals.wait()
    to_smem.wait()
    for cp in (v_sib, s_dn, s_up, s_op):
        cp.wait_recv()

    def p_tile(yr, zr):
        panel = yr * 2 + zr // 4
        for h in range(2):
            row = lax.rem(zr, 4) * 2 + h
            picked = jnp.concatenate([g[csm[panel, row, k]] for k in range(8)], axis=0)
            out = jnp.dot(ball[panel, row], picked, preferred_element_type=F32).astype(BF)
            sl = slice(h * BLOCK, (h + 1) * BLOCK)
            for a in range(NA):
                pa[a, yr, zr, sl] = out[:, a * LANES : (a + 1) * LANES]
            pb[zr, yr, sl] = out[:, NA * LANES :]

    def tiles(n, where):
        def step(i, carry):
            p_tile(*where(i))
            return carry

        lax.fori_loop(0, n, step, 0)

    def y_at(o):
        return lax.rem(yy + o, NY)

    def z_at(o):
        return lax.rem(zz + o, NZ)

    ring_a = [
        Ring(NY, yy, lambda t: (t * NZ + zz, c), pa.at[a], ay.at[a], ay_s.at[a], ay_r.at[a], NZ) for a in range(NA)
    ]
    ring_b = Ring(NZ, zz, lambda t: (yy * NZ + t, c), pb, bz, bz_s, bz_r, NY)

    def both(ring, s):
        for d in range(2):
            ring.start(d, s)

    tiles(NZ, lambda i: (y_at(2), i))
    for a in range(NA):
        both(ring_a[a], 0)
    tiles(NY - 1, lambda i: (y_at(i + 3), z_at(4)))
    both(ring_b, 0)
    tiles(NZ - 1, lambda i: (y_at(1), z_at(i + 5)))
    tiles(NZ - 1, lambda i: (y_at(3), z_at(i + 5)))
    both(ring_a[0], 1)
    tiles(NZ - 1, lambda i: (yy, z_at(i + 5)))
    both(ring_b, 1)
    both(ring_a[1], 1)
    both(ring_b, 2)
    both(ring_a[2], 1)
    both(ring_b, 3)

    az_copies, by_copies = [], []

    def second(a):
        ring_a[a].finish()
        ra[a] = ring_a[a].total().astype(BF)
        az_copies.append(
            [remote(ra.at[a, z_at(o)], az.at[a, o - 1], az_s.at[a, o - 1], az_r.at[a, o - 1], z_peer(o)) for o in range(1, NZ)]
        )
        for cp in az_copies[a]:
            cp.start()

    second(0)
    ring_b.finish()
    rb[...] = ring_b.total().astype(BF)
    for o in range(1, NY):
        by_copies.append(remote(rb.at[y_at(o)], by.at[o - 1], by_s.at[o - 1], by_r.at[o - 1], y_peer(o)))
    for cp in by_copies:
        cp.start()
    for a in range(1, NA):
        second(a)
    scale = 1.0 / (count - 1.0)
    total = rb[yy].astype(F32)
    for o in range(1, NY):
        by_copies[o - 1].wait_recv()
        total = total + by[o - 1].astype(F32)
    cov_ref[:, NA * LANES :] = total * scale
    for a in range(NA):
        total = ra[a, zz].astype(F32)
        for o in range(1, NZ):
            az_copies[a][o - 1].wait_recv()
            total = total + az[a, o - 1].astype(F32)
        cov_ref[:, a * LANES : (a + 1) * LANES] = total * scale

    for ring in (*ring_a, ring_b):
        ring.drain()
    for copies in (*az_copies, by_copies, xz_copies, xy_copies, sz_copies, sy_copies, col_copies):
        for cp in copies:
            cp.wait_send()
    for cp in (v_up, v_dn, v_sib, f_up, f_dn, s_dn, s_up, s_op):
        cp.wait_send()


def on_device(frames, b_values, b_cols, frame_window):
    rows, cart = frames.shape
    vmem = pl.BlockSpec(memory_space=pltpu.VMEM)
    hbm = pl.BlockSpec(memory_space=pl.ANY)
    bdt, cols = pl.pallas_call(
        densify,
        out_shape=(jax.ShapeDtypeStruct((cart, PANEL), BF), jax.ShapeDtypeStruct((8, 128), jnp.int32)),
        in_specs=[pl.BlockSpec(memory_space=pltpu.SMEM), vmem, vmem],
        out_specs=(vmem, vmem),
        name="densify",
    )(b_cols, b_cols, b_values)
    wrow = frame_window.reshape(1, rows)
    dma = pltpu.SemaphoreType.DMA
    count, mean, cov = pl.pallas_call(
        main_kernel,
        out_shape=(
            jax.ShapeDtypeStruct((1, 128), F32),
            jax.ShapeDtypeStruct((1, PANEL), F32),
            jax.ShapeDtypeStruct((OWN, PANEL), F32),
        ),
        in_specs=[hbm, hbm, vmem, vmem, vmem],
        out_specs=(vmem, vmem, vmem),
        scratch_shapes=[
            pltpu.VMEM((rows, cart), BF),
            pltpu.VMEM((cart, PANEL), BF),
            pltpu.VMEM((rows, PANEL), BF),
            pltpu.VMEM((cart // BLOCK, BLOCK, PANEL), BF),
            pltpu.VMEM((NC, 8, BLOCK, PANEL), BF),
            pltpu.VMEM((NC, 8, 128), jnp.int32),
            pltpu.SMEM((NC, 8, 128), jnp.int32),
            pltpu.VMEM((NZ, 1, cart), F32),
            pltpu.VMEM((NY, 1, cart), F32),
            pltpu.VMEM((NZ, 1, PANEL + 128), F32),
            pltpu.VMEM((NY, 1, PANEL + 128), F32),
            pltpu.VMEM((1, cart), F32),
            pltpu.VMEM((NA, NY, NZ, OWN, LANES), BF),
            pltpu.VMEM((NZ, NY, OWN, LANES), BF),
            pltpu.VMEM((NA, NZ, OWN, LANES), BF),
            pltpu.VMEM((NY, OWN, LANES), BF),
            pltpu.VMEM((NA, 2, NY // 2, NZ, OWN, LANES), BF),
            pltpu.VMEM((NA, NZ - 1, OWN, LANES), BF),
            pltpu.VMEM((2, NZ // 2, NY, OWN, LANES), BF),
            pltpu.VMEM((NY - 1, OWN, LANES), BF),
            dma((5,)), dma((2,)), dma((8,)), dma((8,)), dma((7,)), dma((7,)),
            dma((NZ - 1,)), dma((NZ - 1,)), dma((NY - 1,)), dma((NY - 1,)),
            dma((NZ - 1,)), dma((NZ - 1,)), dma((NY - 1,)), dma((NY - 1,)),
            dma((NA, 2, NY // 2)), dma((NA, 2, NY // 2)), dma((NA, NZ - 1)), dma((NA, NZ - 1)),
            dma((2, NZ // 2)), dma((2, NZ // 2)), dma((NY - 1,)), dma((NY - 1,)),
        ],
        compiler_params=pltpu.CompilerParams(
            collective_id=0, has_side_effects=True, vmem_limit_bytes=60 * 1024 * 1024
        ),
        name="covariance",
    )(frames, bdt, b_values.reshape(8, BLOCK, PANEL), cols, wrow)
    return count[0, 0], mean.reshape(PANEL), cov


def solution(mesh):
    return jax.shard_map(
        on_device,
        mesh=mesh,
        in_specs=(P("frame", None), P("coord", None), P("coord", None), P("frame")),
        out_specs=(P(), P("coord"), P("frame", "coord")),
        check_vma=False,
    )
```

```python
import functools

import jax
import jax.numpy as jnp
from jax import lax
from jax.experimental import pallas as pl
from jax.experimental.pallas import tpu as pltpu
from jax.sharding import PartitionSpec as P

BLOCK = 64
NY, NZ, NX = 4, 8, 4
NF, NC = NY * NZ, NX * 2
PANEL = 512
OWN = 128
LANES = 128
NA = 3
UNIT = 72
MESH = pl.DeviceIdType.MESH
BF = jnp.bfloat16
F32 = jnp.float32


def densify(cols_ref, cols_vec_ref, vals_ref, out_ref, wide_cols_ref):
    out_ref[...] = jnp.zeros_like(out_ref)
    wide_cols_ref[:, 0:8] = cols_vec_ref[...]
    wide_cols_ref[:, 8:] = jnp.zeros((8, 120), jnp.int32)
    turned = vals_ref[...].T
    for r in range(8):
        lanes = slice(r * BLOCK, (r + 1) * BLOCK)
        for k in range(8):
            row = pl.multiple_of(cols_ref[r, k] * BLOCK, BLOCK)
            out_ref[pl.ds(row, BLOCK), lanes] = turned[k * BLOCK : (k + 1) * BLOCK, lanes]


def remote(src, dst, send_sem, recv_sem, device):
    return pltpu.make_async_remote_copy(
        src_ref=src, dst_ref=dst, send_sem=send_sem, recv_sem=recv_sem, device_id=device, device_id_type=MESH
    )


class Ring:
    def __init__(self, n, pos, peer, own, recv, send_sems, recv_sems, rows):
        self.n, self.pos, self.own, self.recv = n, pos, own, recv
        self.peer = [peer(lax.rem(pos + 1, n)), peer(lax.rem(pos + n - 1, n))]
        self.send_sems, self.recv_sems, self.rows = send_sems, recv_sems, rows
        self.half = [slice(rows // 2, rows), slice(0, rows // 2)]

    def target(self, d, s):
        steps = self.n // 2 - s
        return lax.rem(self.pos + (steps if d == 0 else self.n - steps), self.n)

    def copy(self, d, s):
        t = self.target(d, s)
        if s == 0:
            src = self.own.at[t, self.half[d]]
            dst = self.recv.at[d, 0, self.half[d]]
        else:
            src = self.recv.at[d, s - 1]
            dst = self.recv.at[d, s]
        return remote(src, dst, self.send_sems.at[d, s], self.recv_sems.at[d, s], self.peer[d])

    def start(self, d, s):
        if s > 0:
            self.copy(d, s - 1).wait_recv()
            t = self.target(d, s)
            buf = self.recv.at[d, s - 1]
            if s == 1:
                h, o = self.half[d], self.half[1 - d]
                buf[h] = (buf[h].astype(F32) + self.own[t, h].astype(F32)).astype(BF)
                buf[o] = self.own[t, o]
            else:
                buf[...] = (buf[...].astype(F32) + self.own[t].astype(F32)).astype(BF)
        self.copy(d, s).start()

    def finish(self):
        last = self.n // 2 - 1
        for d in range(2):
            self.copy(d, last).wait_recv()

    def total(self, sl=slice(None)):
        last = self.n // 2 - 1
        return (
            self.own[self.pos, sl].astype(F32) + self.recv[0, last, sl].astype(F32) + self.recv[1, last, sl].astype(F32)
        )

    def drain(self):
        for d in range(2):
            for s in range(self.n // 2):
                self.copy(d, s).wait_send()


def main_kernel(
    x_hbm, bdt_hbm, vals_ref, cols_ref, wrow_ref,
    count_ref, mean_ref, cov_ref,
    x, bdt, q, g, ball, cbuf, csm, xz, xy, sz, sy, xm, pa, pb, ra, rb, ay, az, bz, by, fr, land,
    ld_sem, loc_sem, val_s, val_r, col_s, col_r, xz_s, xz_r, xy_s, xy_r, z_s, z_r, y_s, y_r,
    ay_s, ay_r, az_s, az_r, bz_s, bz_r, by_s, by_r, fin_s, fin_r,
):
    f, c = lax.axis_index("frame"), lax.axis_index("coord")
    yy, zz = f // NZ, lax.rem(f, NZ)
    xx, kk = c // 2, lax.rem(c, 2)
    rows_total = x.shape[0]
    XT = 4
    xr = rows_total // XT
    loads = [pltpu.make_async_copy(bdt_hbm, bdt, ld_sem.at[0])]
    for i in range(XT):
        sl = pl.ds(i * xr, xr)
        loads.append(pltpu.make_async_copy(x_hbm.at[sl], x.at[sl], ld_sem.at[i + 1]))
    for cp in loads:
        cp.start()

    def coord_peer(o):
        return (f, lax.rem(c + o, NC))

    def z_peer(o):
        return (yy * NZ + lax.rem(zz + o, NZ), c)

    def y_peer(o):
        return (lax.rem(yy + o, NY) * NZ + zz, c)

    x_up = (f, lax.rem(xx + 1, NX) * 2 + kk)
    x_dn = (f, lax.rem(xx + NX - 1, NX) * 2 + kk)
    sib = (f, xx * 2 + 1 - kk)

    barrier = pltpu.get_barrier_semaphore()
    peers = [coord_peer(o) for o in range(1, NC)] + [z_peer(o) for o in range(1, NZ)] + [y_peer(o) for o in range(1, NY)]
    for p in peers:
        pl.semaphore_signal(barrier, inc=1, device_id=p, device_id_type=MESH)
    pl.semaphore_wait(barrier, len(peers))

    c_up, c_dn, c_op = x_up[1], x_dn[1], lax.rem(c + 4, NC)
    lo, hi = pl.ds(0, 4), pl.ds(4, 4)
    own_vals = pltpu.make_async_copy(vals_ref, ball.at[c], loc_sem.at[0])
    own_cols = pltpu.make_async_copy(cols_ref, cbuf.at[c], loc_sem.at[1])
    own_vals.start()
    own_cols.start()
    v_up = remote(vals_ref, ball.at[c], val_s.at[0], val_r.at[0], x_up)
    v_dn = remote(vals_ref, ball.at[c], val_s.at[1], val_r.at[1], x_dn)
    v_sib = remote(vals_ref, ball.at[c], val_s.at[2], val_r.at[2], sib)
    for cp in (v_up, v_dn, v_sib):
        cp.start()
    col_copies = [
        remote(cols_ref, cbuf.at[c], col_s.at[o - 1], col_r.at[o - 1], coord_peer(o)) for o in range(1, NC)
    ]
    for cp in col_copies:
        cp.start()

    loads[0].wait()
    wrow = jnp.broadcast_to(wrow_ref[...].astype(F32), (8, rows_total))
    whalf = wrow.astype(BF)
    sums = jnp.zeros((8, x.shape[1]), F32)

    def project(i):
        sl = slice(i * xr, (i + 1) * xr)
        q[sl] = jnp.dot(x[sl], bdt[...], preferred_element_type=F32).astype(BF)

    for i in range(XT):
        loads[i + 1].wait()
        sl = slice(i * xr, (i + 1) * xr)
        sums = sums + jnp.dot(whalf[:, sl], x[sl], preferred_element_type=F32)
        if i < XT - 1:
            project(i)

    def all_to_all(buf, mine, peer, n, send_sems, recv_sems):
        copies = [remote(buf.at[mine], buf.at[mine], send_sems.at[o - 1], recv_sems.at[o - 1], peer(o)) for o in range(1, n)]
        for cp in copies:
            cp.start()
        return copies

    def gathered(buf, copies):
        for cp in copies:
            cp.wait_recv()
        part = buf[0]
        for j in range(1, buf.shape[0]):
            part = part + buf[j]
        return part

    xz[zz] = sums[0:1]
    xz_copies = all_to_all(xz, zz, z_peer, NZ, xz_s, xz_r)
    project(XT - 1)
    sz[zz, :, :PANEL] = jnp.dot(whalf, q[...], preferred_element_type=F32)[0:1]
    sz[zz, :, PANEL:] = jnp.broadcast_to(jnp.sum(wrow[0:1], axis=1, keepdims=True), (1, 128))
    sz_copies = all_to_all(sz, zz, z_peer, NZ, z_s, z_r)

    xy[yy] = gathered(xz, xz_copies)
    xy_copies = all_to_all(xy, yy, y_peer, NY, xy_s, xy_r)
    sy[yy] = gathered(sz, sz_copies)
    sy_copies = all_to_all(sy, yy, y_peer, NY, y_s, y_r)
    v_up.wait_recv()
    f_up = remote(ball.at[c_dn, hi], ball.at[c_dn, hi], val_s.at[3], val_r.at[3], x_up)
    f_up.start()
    s_dn = remote(ball.at[c_dn], ball.at[c_dn], val_s.at[4], val_r.at[4], sib)
    s_dn.start()
    v_dn.wait_recv()
    f_dn = remote(ball.at[c_up, lo], ball.at[c_up, lo], val_s.at[5], val_r.at[5], x_dn)
    f_dn.start()
    s_up = remote(ball.at[c_up], ball.at[c_up], val_s.at[6], val_r.at[6], sib)
    s_up.start()

    wcol = jnp.broadcast_to(wrow[0:1], (128, rows_total)).T
    whole_x = gathered(xy, xy_copies)
    whole = gathered(sy, sy_copies)
    count_ref[...] = whole[:, PANEL:]
    count = whole[:, PANEL : PANEL + 1]
    mean = whole[:, :PANEL] / count
    mean_ref[...] = mean
    xm[...] = whole_x * (1.0 / count)
    wide = jnp.concatenate([wcol] * (PANEL // 128), axis=1)
    q[...] = (wide * (q[...].astype(F32) - mean)).astype(BF)

    GT = 384

    def g_tile(i, carry):
        start = pl.multiple_of(i * GT, 128)
        moved = (x[:, pl.ds(start, GT)].astype(F32) - xm[:, pl.ds(start, GT)]).astype(BF)
        tile = lax.dot_general(
            moved, q[...], (((0,), (0,)), ((), ())), preferred_element_type=F32
        ).astype(BF)
        for b in range(GT // BLOCK):
            g[i * (GT // BLOCK) + b] = tile[b * BLOCK : (b + 1) * BLOCK]
        return carry

    lax.fori_loop(0, x.shape[1] // GT, g_tile, 0)

    f_up.wait_recv()
    f_dn.wait_recv()
    s_op = remote(ball.at[c_op], ball.at[c_op], val_s.at[7], val_r.at[7], sib)
    s_op.start()
    for cp in col_copies:
        cp.wait_recv()
    own_cols.wait()
    to_smem = pltpu.make_async_copy(cbuf, csm, loc_sem.at[1])
    to_smem.start()
    own_vals.wait()
    to_smem.wait()
    for cp in (v_sib, s_dn, s_up, s_op):
        cp.wait_recv()

    def p_rows(panel, row, lanes):
        picked = jnp.concatenate([g[csm[panel, row, k], :, lanes] for k in range(8)], axis=0)
        return jnp.dot(ball[panel, row], picked, preferred_element_type=F32)

    def keep(j, t, z, rows, value):
        if j < NA:
            pa[j, t, z, rows] = value.astype(BF)
        else:
            pb[z, t, rows] = value.astype(BF)

    def near_blocks(pair):
        def step(z, carry):
            panel = lax.rem(c + z // 2, NC)
            for p in range(2):
                for h in range(2):
                    row = (lax.rem(z, 2) * 2 + p) * 2 + h
                    out = p_rows(panel, row, slice(pair * 256, pair * 256 + 256))
                    for tt in range(2):
                        for jj in range(2):
                            part = out[tt * 32 : tt * 32 + 32, jj * LANES : (jj + 1) * LANES]
                            keep(pair * 2 + jj, 2 * h + tt, z, slice(p * 32, p * 32 + 32), part)
            return carry

        lax.fori_loop(0, NZ, step, 0)

    def far_block(j, e):
        return lax.rem(j + 4 - e - c // 4, 4)

    def far_blocks(j):
        for e in range(2):
            for h in range(2):
                out = p_rows(c_op, far_block(j, e) * 2 + h, slice(j * LANES, (j + 1) * LANES))
                for tt in range(2):
                    for zq in range(4):
                        part = out[tt * 32 + zq * 8 : tt * 32 + zq * 8 + 8]
                        keep(j, 2 * h + tt, 4 * e + zq, slice(64, 72), part)

    def y_at(o):
        return lax.rem(yy + o, NY)

    def z_at(o):
        return lax.rem(zz + o, NZ)

    ring_a = [
        Ring(NY, yy, lambda t: (t * NZ + zz, c), pa.at[a], ay.at[a], ay_s.at[a], ay_r.at[a], NZ) for a in range(NA)
    ]
    ring_b = Ring(NZ, zz, lambda t: (yy * NZ + t, c), pb, bz, bz_s, bz_r, NY)

    def both(ring, s):
        for d in range(2):
            ring.start(d, s)

    near_blocks(0)
    for j in range(2):
        far_blocks(j)
        both(ring_a[j], 0)
    near_blocks(1)
    far_blocks(3)
    both(ring_b, 0)
    far_blocks(2)
    both(ring_a[2], 0)
    both(ring_b, 1)
    both(ring_a[0], 1)
    both(ring_b, 2)
    both(ring_a[1], 1)
    both(ring_b, 3)
    both(ring_a[2], 1)

    az_copies, by_copies = [], []

    def second(a):
        ring_a[a].finish()
        ra[a] = ring_a[a].total().astype(BF)
        az_copies.append(
            [remote(ra.at[a, z_at(o)], az.at[a, o - 1], az_s.at[a, o - 1], az_r.at[a, o - 1], z_peer(o)) for o in range(1, NZ)]
        )
        for cp in az_copies[a]:
            cp.start()

    second(0)
    ring_b.finish()
    rb[...] = ring_b.total().astype(BF)
    for o in range(1, NY):
        by_copies.append(remote(rb.at[y_at(o)], by.at[o - 1], by_s.at[o - 1], by_r.at[o - 1], y_peer(o)))
    for cp in by_copies:
        cp.start()
    for a in range(1, NA):
        second(a)
    scale = 1.0 / (count - 1.0)
    sent = []

    def place(j, n, src, dst_rows, delta, block, mirrored):
        row_panel = lax.rem(c + delta, NC)
        target = row_panel * 4 + block
        dst = land.at[j, dst_rows]
        here = make_local(src, dst, fin_r.at[j])
        there = remote(src, dst, fin_s.at[j, n], fin_r.at[j], (target, c))
        same = target == f

        @pl.when(same)
        def _():
            here.start()

        @pl.when(jnp.logical_not(same))
        def _():
            there.start()

        sent.append((jnp.logical_not(same), there))
        turned = remote(src, land.at[block, dst_rows], fin_s.at[j, n + 3], fin_r.at[block], (c * 4 + j, row_panel))

        @pl.when(mirrored)
        def _():
            turned.start()

        sent.append((mirrored, turned))

    def make_local(src, dst, sem):
        return pltpu.make_async_copy(src, dst, sem)

    def deliver(j, total):
        fr[j] = (total * scale).reshape(UNIT // 8, 8, LANES)
        for p in range(2):
            place(j, p, fr.at[j, pl.ds(4 * p, 4)], pl.ds(4 * yy, 4), zz // 2, lax.rem(zz, 2) * 2 + p, zz >= 2)
        e = zz // 4
        place(j, 2, fr.at[j, pl.ds(8, 1)], pl.ds(4 * yy + lax.rem(zz, 4), 1), 4, far_block(j, e), zz >= 0)

    total = rb[yy].astype(F32)
    for o in range(1, NY):
        by_copies[o - 1].wait_recv()
        total = total + by[o - 1].astype(F32)
    deliver(NA, total)
    for a in range(NA):
        total = ra[a, zz].astype(F32)
        for o in range(1, NZ):
            az_copies[a][o - 1].wait_recv()
            total = total + az[a, o - 1].astype(F32)
        deliver(a, total)

    delta = lax.rem(f // 4 - c + NC, NC)
    for j in range(NA + 1):
        remote(land.at[j], land.at[j], fin_s.at[j, 0], fin_r.at[j], sib).wait_recv()
        block = land[j].reshape(OWN, LANES)
        off = lax.rem(j - lax.rem(f, 4) + 4, 4) - c // 4
        straight = jnp.where(delta == 4, jnp.logical_and(off >= 0, off <= 1), delta < 4)
        cov_ref[:, j * LANES : (j + 1) * LANES] = jnp.where(straight, block, block.T)
    for going, cp in sent:

        @pl.when(going)
        def _(cp=cp):
            cp.wait_send()

    for ring in (*ring_a, ring_b):
        ring.drain()
    for copies in (*az_copies, by_copies, xz_copies, xy_copies, sz_copies, sy_copies, col_copies):
        for cp in copies:
            cp.wait_send()
    for cp in (v_up, v_dn, v_sib, f_up, f_dn, s_dn, s_up, s_op):
        cp.wait_send()


def on_device(frames, b_values, b_cols, frame_window):
    rows, cart = frames.shape
    vmem = pl.BlockSpec(memory_space=pltpu.VMEM)
    hbm = pl.BlockSpec(memory_space=pl.ANY)
    bdt, cols = pl.pallas_call(
        densify,
        out_shape=(jax.ShapeDtypeStruct((cart, PANEL), BF), jax.ShapeDtypeStruct((8, 128), jnp.int32)),
        in_specs=[pl.BlockSpec(memory_space=pltpu.SMEM), vmem, vmem],
        out_specs=(vmem, vmem),
        name="densify",
    )(b_cols, b_cols, b_values)
    wrow = frame_window.reshape(1, rows)
    dma = pltpu.SemaphoreType.DMA
    count, mean, cov = pl.pallas_call(
        main_kernel,
        out_shape=(
            jax.ShapeDtypeStruct((1, 128), F32),
            jax.ShapeDtypeStruct((1, PANEL), F32),
            jax.ShapeDtypeStruct((OWN, PANEL), F32),
        ),
        in_specs=[hbm, hbm, vmem, vmem, vmem],
        out_specs=(vmem, vmem, vmem),
        scratch_shapes=[
            pltpu.VMEM((rows, cart), BF),
            pltpu.VMEM((cart, PANEL), BF),
            pltpu.VMEM((rows, PANEL), BF),
            pltpu.VMEM((cart // BLOCK, BLOCK, PANEL), BF),
            pltpu.VMEM((NC, 8, BLOCK, PANEL), BF),
            pltpu.VMEM((NC, 8, 128), jnp.int32),
            pltpu.SMEM((NC, 8, 128), jnp.int32),
            pltpu.VMEM((NZ, 1, cart), F32),
            pltpu.VMEM((NY, 1, cart), F32),
            pltpu.VMEM((NZ, 1, PANEL + 128), F32),
            pltpu.VMEM((NY, 1, PANEL + 128), F32),
            pltpu.VMEM((1, cart), F32),
            pltpu.VMEM((NA, NY, NZ, UNIT, LANES), BF),
            pltpu.VMEM((NZ, NY, UNIT, LANES), BF),
            pltpu.VMEM((NA, NZ, UNIT, LANES), BF),
            pltpu.VMEM((NY, UNIT, LANES), BF),
            pltpu.VMEM((NA, 2, NY // 2, NZ, UNIT, LANES), BF),
            pltpu.VMEM((NA, NZ - 1, UNIT, LANES), BF),
            pltpu.VMEM((2, NZ // 2, NY, UNIT, LANES), BF),
            pltpu.VMEM((NY - 1, UNIT, LANES), BF),
            pltpu.VMEM((NA + 1, UNIT // 8, 8, LANES), F32),
            pltpu.VMEM((NA + 1, OWN // 8, 8, LANES), F32),
            dma((5,)), dma((2,)), dma((8,)), dma((8,)), dma((7,)), dma((7,)),
            dma((NZ - 1,)), dma((NZ - 1,)), dma((NY - 1,)), dma((NY - 1,)),
            dma((NZ - 1,)), dma((NZ - 1,)), dma((NY - 1,)), dma((NY - 1,)),
            dma((NA, 2, NY // 2)), dma((NA, 2, NY // 2)), dma((NA, NZ - 1)), dma((NA, NZ - 1)),
            dma((2, NZ // 2)), dma((2, NZ // 2)), dma((NY - 1,)), dma((NY - 1,)),
            dma((NA + 1, 6)), dma((NA + 1,)),
        ],
        compiler_params=pltpu.CompilerParams(
            collective_id=0, has_side_effects=True, vmem_limit_bytes=60 * 1024 * 1024
        ),
        name="covariance",
    )(frames, bdt, b_values.reshape(8, BLOCK, PANEL), cols, wrow)
    return count[0, 0], mean.reshape(PANEL), cov


def solution(mesh):
    return jax.shard_map(
        on_device,
        mesh=mesh,
        in_specs=(P("frame", None), P("coord", None), P("coord", None), P("frame")),
        out_specs=(P(), P("coord"), P("frame", "coord")),
        check_vma=False,
    )
```

```python
import functools

import jax
import jax.numpy as jnp
from jax import lax
from jax.experimental import pallas as pl
from jax.experimental.pallas import tpu as pltpu
from jax.sharding import PartitionSpec as P

BLOCK = 64
NY, NZ, NX = 4, 8, 4
NF, NC = NY * NZ, NX * 2
PANEL = 512
OWN = 128
LANES = 128
NA = 3
UNIT = 72
ROW = 640
MESH = pl.DeviceIdType.MESH
BF = jnp.bfloat16
F32 = jnp.float32


def remote(src, dst, send_sem, recv_sem, device):
    return pltpu.make_async_remote_copy(
        src_ref=src, dst_ref=dst, send_sem=send_sem, recv_sem=recv_sem, device_id=device, device_id_type=MESH
    )


class Ring:
    def __init__(self, n, pos, peer, own, recv, send_sems, recv_sems, rows):
        self.n, self.pos, self.own, self.recv = n, pos, own, recv
        self.peer = [peer(lax.rem(pos + 1, n)), peer(lax.rem(pos + n - 1, n))]
        self.send_sems, self.recv_sems, self.rows = send_sems, recv_sems, rows
        self.half = [slice(rows // 2, rows), slice(0, rows // 2)]

    def target(self, d, s):
        steps = self.n // 2 - s
        return lax.rem(self.pos + (steps if d == 0 else self.n - steps), self.n)

    def copy(self, d, s):
        t = self.target(d, s)
        if s == 0:
            src = self.own.at[t, self.half[d]]
            dst = self.recv.at[d, 0, self.half[d]]
        else:
            src = self.recv.at[d, s - 1]
            dst = self.recv.at[d, s]
        return remote(src, dst, self.send_sems.at[d, s], self.recv_sems.at[d, s], self.peer[d])

    def start(self, d, s):
        if s > 0:
            self.copy(d, s - 1).wait_recv()
            t = self.target(d, s)
            buf = self.recv.at[d, s - 1]
            if s == 1:
                h, o = self.half[d], self.half[1 - d]
                buf[h] = (buf[h].astype(F32) + self.own[t, h].astype(F32)).astype(BF)
                buf[o] = self.own[t, o]
            else:
                buf[...] = (buf[...].astype(F32) + self.own[t].astype(F32)).astype(BF)
        self.copy(d, s).start()

    def finish(self):
        last = self.n // 2 - 1
        for d in range(2):
            self.copy(d, last).wait_recv()

    def total(self, sl=slice(None)):
        last = self.n // 2 - 1
        return (
            self.own[self.pos, sl].astype(F32) + self.recv[0, last, sl].astype(F32) + self.recv[1, last, sl].astype(F32)
        )

    def drain(self):
        for d in range(2):
            for s in range(self.n // 2):
                self.copy(d, s).wait_send()


def main_kernel(
    x_hbm, vals_ref, cols_ref, wrow_ref,
    count_ref, mean_ref, cov_ref,
    x, vt, found, where_sm, bdt, q, g, ball, cbuf, csm, rows8, xz, xy, sz, sy, xm, pa, pb, ra, rb, ay, az, bz, by, fr, land,
    ld_sem, loc_sem, val_s, val_r, col_s, col_r, xz_s, xz_r, xy_s, xy_r, z_s, z_r, y_s, y_r,
    ay_s, ay_r, az_s, az_r, bz_s, bz_r, by_s, by_r, fin_s, fin_r,
):
    f, c = lax.axis_index("frame"), lax.axis_index("coord")
    yy, zz = f // NZ, lax.rem(f, NZ)
    xx, kk = c // 2, lax.rem(c, 2)
    rows_total = x.shape[0]
    XT = 4
    xr = rows_total // XT
    loads = []
    for i in range(XT):
        sl = pl.ds(i * xr, xr)
        loads.append(pltpu.make_async_copy(x_hbm.at[sl], x.at[sl], ld_sem.at[i]))
    for cp in loads:
        cp.start()

    def coord_peer(o):
        return (f, lax.rem(c + o, NC))

    def z_peer(o):
        return (yy * NZ + lax.rem(zz + o, NZ), c)

    def y_peer(o):
        return (lax.rem(yy + o, NY) * NZ + zz, c)

    x_up = (f, lax.rem(xx + 1, NX) * 2 + kk)
    x_dn = (f, lax.rem(xx + NX - 1, NX) * 2 + kk)
    sib = (f, xx * 2 + 1 - kk)

    barrier = pltpu.get_barrier_semaphore()
    peers = [coord_peer(o) for o in range(1, NC)] + [z_peer(o) for o in range(1, NZ)] + [y_peer(o) for o in range(1, NY)]
    for p in peers:
        pl.semaphore_signal(barrier, inc=1, device_id=p, device_id_type=MESH)
    pl.semaphore_wait(barrier, len(peers))

    c_up, c_dn, c_op = x_up[1], x_dn[1], lax.rem(c + 4, NC)
    lo, hi = pl.ds(0, 4), pl.ds(4, 4)
    own_vals = pltpu.make_async_copy(vals_ref, ball.at[c], loc_sem.at[0])
    own_vals.start()
    cbuf[c, :, 0:8] = cols_ref[...]
    cbuf[c, :, 8:] = jnp.zeros((8, 120), jnp.int32)
    v_up = remote(vals_ref, ball.at[c], val_s.at[0], val_r.at[0], x_up)
    v_dn = remote(vals_ref, ball.at[c], val_s.at[1], val_r.at[1], x_dn)
    v_sib = remote(vals_ref, ball.at[c], val_s.at[2], val_r.at[2], sib)
    for cp in (v_up, v_dn, v_sib):
        cp.start()
    col_copies = [
        remote(cbuf.at[c], cbuf.at[c], col_s.at[o - 1], col_r.at[o - 1], coord_peer(o)) for o in range(1, NC)
    ]
    for cp in col_copies:
        cp.start()

    lane = lax.broadcasted_iota(jnp.int32, (8, 128), 1)
    holder = jnp.full((8, 128), 8, jnp.int32)
    for k in range(8):
        holder = jnp.where(cols_ref[:, k : k + 1] == lane, k, holder)
    found[...] = holder
    to_where = pltpu.make_async_copy(found, where_sm, loc_sem.at[2])
    to_where.start()
    vt[0:8] = vals_ref[...].reshape(PANEL, PANEL).T.reshape(8, BLOCK, PANEL)
    vt[8] = jnp.zeros((BLOCK, PANEL), BF)
    to_where.wait()

    def spread(b, carry):
        for r in range(8):
            lanes = slice(r * BLOCK, (r + 1) * BLOCK)
            bdt[b, :, lanes] = vt[where_sm[r, b], :, lanes]
        return carry

    lax.fori_loop(0, bdt.shape[0], spread, 0)
    wrow = jnp.broadcast_to(wrow_ref[...].astype(F32), (8, rows_total))
    whalf = wrow.astype(BF)
    sums = jnp.zeros((8, x.shape[1]), F32)

    def project(i):
        sl = slice(i * xr, (i + 1) * xr)
        q[sl] = jnp.dot(x[sl], bdt[...].reshape(x.shape[1], PANEL), preferred_element_type=F32).astype(BF)

    cart = x.shape[1]
    for i in range(XT):
        loads[i].wait()
        sl = slice(i * xr, (i + 1) * xr)
        sums = sums + jnp.dot(whalf[:, sl], x[sl], preferred_element_type=F32)
        if i < XT - 1:
            project(i)

    def all_to_all(buf, mine, peer, n, send_sems, recv_sems):
        copies = [remote(buf.at[mine], buf.at[mine], send_sems.at[o - 1], recv_sems.at[o - 1], peer(o)) for o in range(1, n)]
        for cp in copies:
            cp.start()
        return copies

    def gathered(buf, copies):
        for cp in copies:
            cp.wait_recv()
        part = buf[0].astype(F32)
        for j in range(1, buf.shape[0]):
            part = part + buf[j].astype(F32)
        return part

    wide_sums = jnp.concatenate([sums[0:1], jnp.zeros((1, 8 * ROW - cart), F32)], axis=1)
    for i in range(8):
        rows8[i : i + 1] = wide_sums[:, i * ROW : (i + 1) * ROW]
    xz[zz] = rows8[...].astype(BF)
    xz_copies = all_to_all(xz, zz, z_peer, NZ, xz_s, xz_r)
    project(XT - 1)
    sz[zz, :, :PANEL] = jnp.dot(whalf, q[...], preferred_element_type=F32)[0:1]
    sz[zz, :, PANEL:] = jnp.broadcast_to(jnp.sum(wrow[0:1], axis=1, keepdims=True), (1, 128))
    sz_copies = all_to_all(sz, zz, z_peer, NZ, z_s, z_r)

    xy[yy] = gathered(xz, xz_copies).astype(BF)
    xy_copies = all_to_all(xy, yy, y_peer, NY, xy_s, xy_r)
    sy[yy] = gathered(sz, sz_copies)
    sy_copies = all_to_all(sy, yy, y_peer, NY, y_s, y_r)
    v_up.wait_recv()
    f_up = remote(ball.at[c_dn, hi], ball.at[c_dn, hi], val_s.at[3], val_r.at[3], x_up)
    f_up.start()
    s_dn = remote(ball.at[c_dn], ball.at[c_dn], val_s.at[4], val_r.at[4], sib)
    s_dn.start()
    v_dn.wait_recv()
    f_dn = remote(ball.at[c_up, lo], ball.at[c_up, lo], val_s.at[5], val_r.at[5], x_dn)
    f_dn.start()
    s_up = remote(ball.at[c_up], ball.at[c_up], val_s.at[6], val_r.at[6], sib)
    s_up.start()

    wcol = jnp.broadcast_to(wrow[0:1], (128, rows_total)).T
    whole_x = gathered(xy, xy_copies)
    whole = gathered(sy, sy_copies)
    count_ref[...] = whole[:, PANEL:]
    count = whole[:, PANEL : PANEL + 1]
    mean = whole[:, :PANEL] / count
    mean_ref[...] = mean
    whole_x = whole_x * (1.0 / count)
    for i in range(8):
        width = min(ROW, cart - i * ROW)
        if width > 0:
            xm[:, i * ROW : i * ROW + width] = whole_x[i : i + 1, :width]
    wide = jnp.concatenate([wcol] * (PANEL // 128), axis=1)
    q[...] = (wide * (q[...].astype(F32) - mean)).astype(BF)

    GT = 384

    def g_tile(i, carry):
        start = pl.multiple_of(i * GT, 128)
        moved = (x[:, pl.ds(start, GT)].astype(F32) - xm[:, pl.ds(start, GT)]).astype(BF)
        tile = lax.dot_general(
            moved, q[...], (((0,), (0,)), ((), ())), preferred_element_type=F32
        ).astype(BF)
        for b in range(GT // BLOCK):
            g[i * (GT // BLOCK) + b] = tile[b * BLOCK : (b + 1) * BLOCK]
        return carry

    lax.fori_loop(0, x.shape[1] // GT, g_tile, 0)

    f_up.wait_recv()
    f_dn.wait_recv()
    s_op = remote(ball.at[c_op], ball.at[c_op], val_s.at[7], val_r.at[7], sib)
    s_op.start()
    for cp in col_copies:
        cp.wait_recv()
    to_smem = pltpu.make_async_copy(cbuf, csm, loc_sem.at[1])
    to_smem.start()
    own_vals.wait()
    to_smem.wait()
    for cp in (v_sib, s_dn, s_up, s_op):
        cp.wait_recv()

    def p_rows(panel, row, lanes):
        picked = jnp.concatenate([g[csm[panel, row, k], :, lanes] for k in range(8)], axis=0)
        return jnp.dot(ball[panel, row], picked, preferred_element_type=F32)

    def keep(j, t, z, rows, value):
        if j < NA:
            pa[j, t, z, rows] = value.astype(BF)
        else:
            pb[z, t, rows] = value.astype(BF)

    def near_blocks(pair):
        def step(z, carry):
            panel = lax.rem(c + z // 2, NC)
            for p in range(2):
                for h in range(2):
                    row = (lax.rem(z, 2) * 2 + p) * 2 + h
                    out = p_rows(panel, row, slice(pair * 256, pair * 256 + 256))
                    for tt in range(2):
                        for jj in range(2):
                            part = out[tt * 32 : tt * 32 + 32, jj * LANES : (jj + 1) * LANES]
                            keep(pair * 2 + jj, 2 * h + tt, z, slice(p * 32, p * 32 + 32), part)
            return carry

        lax.fori_loop(0, NZ, step, 0)

    def far_block(j, e):
        return lax.rem(j + 4 - e - c // 4, 4)

    def far_blocks(j):
        for e in range(2):
            for h in range(2):
                out = p_rows(c_op, far_block(j, e) * 2 + h, slice(j * LANES, (j + 1) * LANES))
                for tt in range(2):
                    for zq in range(4):
                        part = out[tt * 32 + zq * 8 : tt * 32 + zq * 8 + 8]
                        keep(j, 2 * h + tt, 4 * e + zq, slice(64, 72), part)

    def y_at(o):
        return lax.rem(yy + o, NY)

    def z_at(o):
        return lax.rem(zz + o, NZ)

    ring_a = [
        Ring(NY, yy, lambda t: (t * NZ + zz, c), pa.at[a], ay.at[a], ay_s.at[a], ay_r.at[a], NZ) for a in range(NA)
    ]
    ring_b = Ring(NZ, zz, lambda t: (yy * NZ + t, c), pb, bz, bz_s, bz_r, NY)

    def both(ring, s):
        for d in range(2):
            ring.start(d, s)

    near_blocks(0)
    for j in range(2):
        far_blocks(j)
        both(ring_a[j], 0)
    near_blocks(1)
    far_blocks(3)
    both(ring_b, 0)
    far_blocks(2)
    both(ring_a[2], 0)
    both(ring_b, 1)
    both(ring_a[0], 1)
    both(ring_b, 2)
    both(ring_a[1], 1)
    both(ring_b, 3)
    both(ring_a[2], 1)

    az_copies, by_copies = [], []

    def second(a):
        ring_a[a].finish()
        ra[a] = ring_a[a].total().astype(BF)
        az_copies.append(
            [remote(ra.at[a, z_at(o)], az.at[a, o - 1], az_s.at[a, o - 1], az_r.at[a, o - 1], z_peer(o)) for o in range(1, NZ)]
        )
        for cp in az_copies[a]:
            cp.start()

    second(0)
    ring_b.finish()
    rb[...] = ring_b.total().astype(BF)
    for o in range(1, NY):
        by_copies.append(remote(rb.at[y_at(o)], by.at[o - 1], by_s.at[o - 1], by_r.at[o - 1], y_peer(o)))
    for cp in by_copies:
        cp.start()
    for a in range(1, NA):
        second(a)
    scale = 1.0 / (count - 1.0)
    sent = []

    def place(j, n, src, dst_rows, delta, block, mirrored):
        row_panel = lax.rem(c + delta, NC)
        target = row_panel * 4 + block
        dst = land.at[j, dst_rows]
        here = make_local(src, dst, fin_r.at[j])
        there = remote(src, dst, fin_s.at[j, n], fin_r.at[j], (target, c))
        same = target == f

        @pl.when(same)
        def _():
            here.start()

        @pl.when(jnp.logical_not(same))
        def _():
            there.start()

        sent.append((jnp.logical_not(same), there))
        turned = remote(src, land.at[block, dst_rows], fin_s.at[j, n + 3], fin_r.at[block], (c * 4 + j, row_panel))

        @pl.when(mirrored)
        def _():
            turned.start()

        sent.append((mirrored, turned))

    def make_local(src, dst, sem):
        return pltpu.make_async_copy(src, dst, sem)

    def deliver(j, total):
        fr[j] = (total * scale).reshape(UNIT // 8, 8, LANES)
        for p in range(2):
            place(j, p, fr.at[j, pl.ds(4 * p, 4)], pl.ds(4 * yy, 4), zz // 2, lax.rem(zz, 2) * 2 + p, zz >= 2)
        e = zz // 4
        place(j, 2, fr.at[j, pl.ds(8, 1)], pl.ds(4 * yy + lax.rem(zz, 4), 1), 4, far_block(j, e), zz >= 0)

    total = rb[yy].astype(F32)
    for o in range(1, NY):
        by_copies[o - 1].wait_recv()
        total = total + by[o - 1].astype(F32)
    deliver(NA, total)
    for a in range(NA):
        total = ra[a, zz].astype(F32)
        for o in range(1, NZ):
            az_copies[a][o - 1].wait_recv()
            total = total + az[a, o - 1].astype(F32)
        deliver(a, total)

    delta = lax.rem(f // 4 - c + NC, NC)
    for j in range(NA + 1):
        remote(land.at[j], land.at[j], fin_s.at[j, 0], fin_r.at[j], sib).wait_recv()
        block = land[j].reshape(OWN, LANES)
        off = lax.rem(j - lax.rem(f, 4) + 4, 4) - c // 4
        straight = jnp.where(delta == 4, jnp.logical_and(off >= 0, off <= 1), delta < 4)
        cov_ref[:, j * LANES : (j + 1) * LANES] = jnp.where(straight, block, block.T)
    for going, cp in sent:

        @pl.when(going)
        def _(cp=cp):
            cp.wait_send()

    for ring in (*ring_a, ring_b):
        ring.drain()
    for copies in (*az_copies, by_copies, xz_copies, xy_copies, sz_copies, sy_copies, col_copies):
        for cp in copies:
            cp.wait_send()
    for cp in (v_up, v_dn, v_sib, f_up, f_dn, s_dn, s_up, s_op):
        cp.wait_send()


def on_device(frames, b_values, b_cols, frame_window):
    rows, cart = frames.shape
    vmem = pl.BlockSpec(memory_space=pltpu.VMEM)
    hbm = pl.BlockSpec(memory_space=pl.ANY)
    wrow = frame_window.reshape(1, rows)
    dma = pltpu.SemaphoreType.DMA
    count, mean, cov = pl.pallas_call(
        main_kernel,
        out_shape=(
            jax.ShapeDtypeStruct((1, 128), F32),
            jax.ShapeDtypeStruct((1, PANEL), F32),
            jax.ShapeDtypeStruct((OWN, PANEL), F32),
        ),
        in_specs=[hbm, vmem, vmem, vmem],
        out_specs=(vmem, vmem, vmem),
        scratch_shapes=[
            pltpu.VMEM((rows, cart), BF),
            pltpu.VMEM((9, BLOCK, PANEL), BF),
            pltpu.VMEM((8, 128), jnp.int32),
            pltpu.SMEM((8, 128), jnp.int32),
            pltpu.VMEM((cart // BLOCK, BLOCK, PANEL), BF),
            pltpu.VMEM((rows, PANEL), BF),
            pltpu.VMEM((cart // BLOCK, BLOCK, PANEL), BF),
            pltpu.VMEM((NC, 8, BLOCK, PANEL), BF),
            pltpu.VMEM((NC, 8, 128), jnp.int32),
            pltpu.SMEM((NC, 8, 128), jnp.int32),
            pltpu.VMEM((8, ROW), F32),
            pltpu.VMEM((NZ, 8, ROW), BF),
            pltpu.VMEM((NY, 8, ROW), BF),
            pltpu.VMEM((NZ, 1, PANEL + 128), F32),
            pltpu.VMEM((NY, 1, PANEL + 128), F32),
            pltpu.VMEM((1, cart), F32),
            pltpu.VMEM((NA, NY, NZ, UNIT, LANES), BF),
            pltpu.VMEM((NZ, NY, UNIT, LANES), BF),
            pltpu.VMEM((NA, NZ, UNIT, LANES), BF),
            pltpu.VMEM((NY, UNIT, LANES), BF),
            pltpu.VMEM((NA, 2, NY // 2, NZ, UNIT, LANES), BF),
            pltpu.VMEM((NA, NZ - 1, UNIT, LANES), BF),
            pltpu.VMEM((2, NZ // 2, NY, UNIT, LANES), BF),
            pltpu.VMEM((NY - 1, UNIT, LANES), BF),
            pltpu.VMEM((NA + 1, UNIT // 8, 8, LANES), F32),
            pltpu.VMEM((NA + 1, OWN // 8, 8, LANES), F32),
            dma((4,)), dma((3,)), dma((8,)), dma((8,)), dma((7,)), dma((7,)),
            dma((NZ - 1,)), dma((NZ - 1,)), dma((NY - 1,)), dma((NY - 1,)),
            dma((NZ - 1,)), dma((NZ - 1,)), dma((NY - 1,)), dma((NY - 1,)),
            dma((NA, 2, NY // 2)), dma((NA, 2, NY // 2)), dma((NA, NZ - 1)), dma((NA, NZ - 1)),
            dma((2, NZ // 2)), dma((2, NZ // 2)), dma((NY - 1,)), dma((NY - 1,)),
            dma((NA + 1, 6)), dma((NA + 1,)),
        ],
        compiler_params=pltpu.CompilerParams(
            collective_id=0, has_side_effects=True, vmem_limit_bytes=60 * 1024 * 1024
        ),
        name="covariance",
    )(frames, b_values.reshape(8, BLOCK, PANEL), b_cols, wrow)
    return count[0, 0], mean.reshape(PANEL), cov


def solution(mesh):
    return jax.shard_map(
        on_device,
        mesh=mesh,
        in_specs=(P("frame", None), P("coord", None), P("coord", None), P("frame")),
        out_specs=(P(), P("coord"), P("frame", "coord")),
        check_vma=False,
    )
```

```python
import functools

import jax
import jax.numpy as jnp
from jax import lax
from jax.experimental import pallas as pl
from jax.experimental.pallas import tpu as pltpu
from jax.sharding import PartitionSpec as P

BLOCK = 64
NY, NZ, NX = 4, 8, 4
NF, NC = NY * NZ, NX * 2
PANEL = 512
OWN = 128
LANES = 128
NA = 3
UNIT = 72
ROW = 640
MESH = pl.DeviceIdType.MESH
BF = jnp.bfloat16
F32 = jnp.float32


def remote(src, dst, send_sem, recv_sem, device):
    return pltpu.make_async_remote_copy(
        src_ref=src, dst_ref=dst, send_sem=send_sem, recv_sem=recv_sem, device_id=device, device_id_type=MESH
    )


class Ring:
    def __init__(self, n, pos, peer, own, recv, send_sems, recv_sems, rows):
        self.n, self.pos, self.own, self.recv = n, pos, own, recv
        self.peer = [peer(lax.rem(pos + 1, n)), peer(lax.rem(pos + n - 1, n))]
        self.send_sems, self.recv_sems, self.rows = send_sems, recv_sems, rows
        self.half = [slice(rows // 2, rows), slice(0, rows // 2)]

    def target(self, d, s):
        steps = self.n // 2 - s
        return lax.rem(self.pos + (steps if d == 0 else self.n - steps), self.n)

    def copy(self, d, s):
        t = self.target(d, s)
        if s == 0:
            src = self.own.at[t, self.half[d]]
            dst = self.recv.at[d, 0, self.half[d]]
        else:
            src = self.recv.at[d, s - 1]
            dst = self.recv.at[d, s]
        return remote(src, dst, self.send_sems.at[d, s], self.recv_sems.at[d, s], self.peer[d])

    def start(self, d, s):
        if s > 0:
            self.copy(d, s - 1).wait_recv()
            t = self.target(d, s)
            buf = self.recv.at[d, s - 1]
            if s == 1:
                h, o = self.half[d], self.half[1 - d]
                buf[h] = (buf[h].astype(F32) + self.own[t, h].astype(F32)).astype(BF)
                buf[o] = self.own[t, o]
            else:
                buf[...] = (buf[...].astype(F32) + self.own[t].astype(F32)).astype(BF)
        self.copy(d, s).start()

    def finish(self):
        last = self.n // 2 - 1
        for d in range(2):
            self.copy(d, last).wait_recv()

    def total(self, sl=slice(None)):
        last = self.n // 2 - 1
        return (
            self.own[self.pos, sl].astype(F32) + self.recv[0, last, sl].astype(F32) + self.recv[1, last, sl].astype(F32)
        )

    def drain(self):
        for d in range(2):
            for s in range(self.n // 2):
                self.copy(d, s).wait_send()


def main_kernel(
    x_hbm, vals_ref, cols_ref, wrow_ref,
    count_ref, mean_ref, cov_ref,
    x, vt, found, where_sm, bdt, q, g, ball, cbuf, csm, rows8, xz, xy, sz, sy, xm, pa, pb, ra, rb, ay, az, bz, by, fr, land,
    ld_sem, loc_sem, val_s, val_r, col_s, col_r, xz_s, xz_r, xy_s, xy_r, z_s, z_r, y_s, y_r,
    ay_s, ay_r, az_s, az_r, bz_s, bz_r, by_s, by_r, fin_s, fin_r,
):
    f, c = lax.axis_index("frame"), lax.axis_index("coord")
    yy, zz = f // NZ, lax.rem(f, NZ)
    xx, kk = c // 2, lax.rem(c, 2)
    rows_total = x.shape[0]
    XT = 4
    xr = rows_total // XT
    loads = []
    for i in range(XT):
        sl = pl.ds(i * xr, xr)
        loads.append(pltpu.make_async_copy(x_hbm.at[sl], x.at[sl], ld_sem.at[i]))
    for cp in loads:
        cp.start()

    def coord_peer(o):
        return (f, lax.rem(c + o, NC))

    def z_peer(o):
        return (yy * NZ + lax.rem(zz + o, NZ), c)

    def y_peer(o):
        return (lax.rem(yy + o, NY) * NZ + zz, c)

    x_up = (f, lax.rem(xx + 1, NX) * 2 + kk)
    x_dn = (f, lax.rem(xx + NX - 1, NX) * 2 + kk)
    sib = (f, xx * 2 + 1 - kk)

    barrier = pltpu.get_barrier_semaphore()
    peers = [coord_peer(o) for o in range(1, NC)] + [z_peer(o) for o in range(1, NZ)] + [y_peer(o) for o in range(1, NY)]
    for p in peers:
        pl.semaphore_signal(barrier, inc=1, device_id=p, device_id_type=MESH)
    pl.semaphore_wait(barrier, len(peers))

    c_up, c_dn, c_op = x_up[1], x_dn[1], lax.rem(c + 4, NC)
    lo, hi = pl.ds(0, 3), pl.ds(3, 5)
    own_vals = pltpu.make_async_copy(vals_ref, ball.at[c], loc_sem.at[0])
    own_vals.start()
    cbuf[c, :, 0:8] = cols_ref[...]
    cbuf[c, :, 8:] = jnp.zeros((8, 120), jnp.int32)
    v_up = remote(vals_ref.at[hi], ball.at[c, hi], val_s.at[0], val_r.at[0], x_up)
    v_dn = remote(vals_ref.at[lo], ball.at[c, lo], val_s.at[1], val_r.at[1], x_dn)
    v_dn_rest = remote(vals_ref.at[hi], ball.at[c, hi], val_s.at[4], val_r.at[4], x_dn)
    v_sib = remote(vals_ref, ball.at[c], val_s.at[2], val_r.at[2], sib)
    for cp in (v_up, v_dn, v_dn_rest, v_sib):
        cp.start()
    col_copies = [
        remote(cbuf.at[c], cbuf.at[c], col_s.at[o - 1], col_r.at[o - 1], coord_peer(o)) for o in range(1, NC)
    ]
    for cp in col_copies:
        cp.start()

    lane = lax.broadcasted_iota(jnp.int32, (8, 128), 1)
    holder = jnp.full((8, 128), 8, jnp.int32)
    for k in range(8):
        holder = jnp.where(cols_ref[:, k : k + 1] == lane, k, holder)
    found[...] = holder
    to_where = pltpu.make_async_copy(found, where_sm, loc_sem.at[2])
    to_where.start()
    vt[0:8] = vals_ref[...].reshape(PANEL, PANEL).T.reshape(8, BLOCK, PANEL)
    vt[8] = jnp.zeros((BLOCK, PANEL), BF)
    to_where.wait()

    def spread(b, carry):
        for r in range(8):
            lanes = slice(r * BLOCK, (r + 1) * BLOCK)
            bdt[b, :, lanes] = vt[where_sm[r, b], :, lanes]
        return carry

    lax.fori_loop(0, bdt.shape[0], spread, 0)
    wrow = jnp.broadcast_to(wrow_ref[...].astype(F32), (8, rows_total))
    whalf = wrow.astype(BF)
    sums = jnp.zeros((8, x.shape[1]), F32)

    def project(i):
        sl = slice(i * xr, (i + 1) * xr)
        q[sl] = jnp.dot(x[sl], bdt[...].reshape(x.shape[1], PANEL), preferred_element_type=F32).astype(BF)

    cart = x.shape[1]
    for i in range(XT):
        loads[i].wait()
        sl = slice(i * xr, (i + 1) * xr)
        sums = sums + jnp.dot(whalf[:, sl], x[sl], preferred_element_type=F32)
        if i < XT - 1:
            project(i)

    def all_to_all(buf, mine, peer, n, send_sems, recv_sems):
        copies = [remote(buf.at[mine], buf.at[mine], send_sems.at[o - 1], recv_sems.at[o - 1], peer(o)) for o in range(1, n)]
        for cp in copies:
            cp.start()
        return copies

    def gathered(buf, copies):
        for cp in copies:
            cp.wait_recv()
        part = buf[0].astype(F32)
        for j in range(1, buf.shape[0]):
            part = part + buf[j].astype(F32)
        return part

    wide_sums = jnp.concatenate([sums[0:1], jnp.zeros((1, 8 * ROW - cart), F32)], axis=1)
    for i in range(8):
        rows8[i : i + 1] = wide_sums[:, i * ROW : (i + 1) * ROW]
    xz[zz] = rows8[...].astype(BF)
    xz_copies = all_to_all(xz, zz, z_peer, NZ, xz_s, xz_r)
    project(XT - 1)
    sz[zz, :, :PANEL] = jnp.dot(whalf, q[...], preferred_element_type=F32)[0:1]
    sz[zz, :, PANEL:] = jnp.broadcast_to(jnp.sum(wrow[0:1], axis=1, keepdims=True), (1, 128))
    sz_copies = all_to_all(sz, zz, z_peer, NZ, z_s, z_r)

    v_up.wait_recv()
    f_up = remote(ball.at[c_dn, hi], ball.at[c_dn, hi], val_s.at[3], val_r.at[3], x_up)
    f_up.start()
    v_dn.wait_recv()
    f_dn = remote(ball.at[c_up, lo], ball.at[c_up, lo], val_s.at[5], val_r.at[5], x_dn)
    f_dn.start()

    xy[yy] = gathered(xz, xz_copies).astype(BF)
    xy_copies = all_to_all(xy, yy, y_peer, NY, xy_s, xy_r)
    sy[yy] = gathered(sz, sz_copies)
    sy_copies = all_to_all(sy, yy, y_peer, NY, y_s, y_r)
    wcol = jnp.broadcast_to(wrow[0:1], (128, rows_total)).T
    v_dn_rest.wait_recv()
    s_up = remote(ball.at[c_up], ball.at[c_up], val_s.at[6], val_r.at[6], sib)
    s_up.start()
    whole_x = gathered(xy, xy_copies)
    whole = gathered(sy, sy_copies)
    count_ref[...] = whole[:, PANEL:]
    count = whole[:, PANEL : PANEL + 1]
    mean = whole[:, :PANEL] / count
    mean_ref[...] = mean
    whole_x = whole_x * (1.0 / count)
    for i in range(8):
        width = min(ROW, cart - i * ROW)
        if width > 0:
            xm[:, i * ROW : i * ROW + width] = whole_x[i : i + 1, :width]
    wide = jnp.concatenate([wcol] * (PANEL // 128), axis=1)
    q[...] = (wide * (q[...].astype(F32) - mean)).astype(BF)

    GT = 384

    def g_tile(i, carry):
        start = pl.multiple_of(i * GT, 128)
        moved = (x[:, pl.ds(start, GT)].astype(F32) - xm[:, pl.ds(start, GT)]).astype(BF)
        tile = lax.dot_general(
            moved, q[...], (((0,), (0,)), ((), ())), preferred_element_type=F32
        ).astype(BF)
        for b in range(GT // BLOCK):
            g[i * (GT // BLOCK) + b] = tile[b * BLOCK : (b + 1) * BLOCK]
        return carry

    g_tiles = x.shape[1] // GT
    lax.fori_loop(0, g_tiles - 3, g_tile, 0)

    f_up.wait_recv()
    f_dn.wait_recv()
    s_op = remote(ball.at[c_op], ball.at[c_op], val_s.at[7], val_r.at[7], sib)

    @pl.when(kk == 0)
    def _():
        s_op.start()

    lax.fori_loop(g_tiles - 3, g_tiles, g_tile, 0)
    for cp in col_copies:
        cp.wait_recv()
    to_smem = pltpu.make_async_copy(cbuf, csm, loc_sem.at[1])
    to_smem.start()
    own_vals.wait()
    to_smem.wait()
    for cp in (v_sib, s_up):
        cp.wait_recv()

    @pl.when(kk == 1)
    def _():
        remote(ball.at[c_op - 1], ball.at[c_op - 1], val_s.at[7], val_r.at[7], sib).wait_recv()

    def p_rows(panel, row, lanes):
        picked = jnp.concatenate([g[csm[panel, row, k], :, lanes] for k in range(8)], axis=0)
        return jnp.dot(ball[panel, row], picked, preferred_element_type=F32)

    def keep(j, t, z, rows, value):
        if j < NA:
            pa[j, t, z, rows] = value.astype(BF)
        else:
            pb[z, t, rows] = value.astype(BF)

    def near_blocks(pair):
        def step(z, carry):
            panel = lax.rem(c + z // 2, NC)
            for p in range(2):
                for h in range(2):
                    row = (lax.rem(z, 2) * 2 + p) * 2 + h
                    out = p_rows(panel, row, slice(pair * 256, pair * 256 + 256))
                    for tt in range(2):
                        for jj in range(2):
                            part = out[tt * 32 : tt * 32 + 32, jj * LANES : (jj + 1) * LANES]
                            keep(pair * 2 + jj, 2 * h + tt, z, slice(p * 32, p * 32 + 32), part)
            return carry

        lax.fori_loop(0, NZ, step, 0)

    def far_block(j, e):
        return lax.rem(j + 4 - e - c // 4, 4)

    def far_blocks(j):
        for e in range(2):
            for h in range(2):
                out = p_rows(c_op, far_block(j, e) * 2 + h, slice(j * LANES, (j + 1) * LANES))
                for tt in range(2):
                    for zq in range(4):
                        part = out[tt * 32 + zq * 8 : tt * 32 + zq * 8 + 8]
                        keep(j, 2 * h + tt, 4 * e + zq, slice(64, 72), part)

    def y_at(o):
        return lax.rem(yy + o, NY)

    def z_at(o):
        return lax.rem(zz + o, NZ)

    ring_a = [
        Ring(NY, yy, lambda t: (t * NZ + zz, c), pa.at[a], ay.at[a], ay_s.at[a], ay_r.at[a], NZ) for a in range(NA)
    ]
    ring_b = Ring(NZ, zz, lambda t: (yy * NZ + t, c), pb, bz, bz_s, bz_r, NY)

    def both(ring, s):
        for d in range(2):
            ring.start(d, s)

    near_blocks(0)
    for j in range(2):
        far_blocks(j)
        both(ring_a[j], 0)
    near_blocks(1)
    far_blocks(3)
    both(ring_b, 0)
    far_blocks(2)
    both(ring_a[2], 0)
    both(ring_b, 1)
    both(ring_a[0], 1)
    both(ring_b, 2)
    both(ring_a[1], 1)
    both(ring_b, 3)
    both(ring_a[2], 1)

    az_copies, by_copies = [], []

    def second(a):
        ring_a[a].finish()
        ra[a] = ring_a[a].total().astype(BF)
        az_copies.append(
            [remote(ra.at[a, z_at(o)], az.at[a, o - 1], az_s.at[a, o - 1], az_r.at[a, o - 1], z_peer(o)) for o in range(1, NZ)]
        )
        for cp in az_copies[a]:
            cp.start()

    second(0)
    ring_b.finish()
    rb[...] = ring_b.total().astype(BF)
    for o in range(1, NY):
        by_copies.append(remote(rb.at[y_at(o)], by.at[o - 1], by_s.at[o - 1], by_r.at[o - 1], y_peer(o)))
    for cp in by_copies:
        cp.start()
    for a in range(1, NA):
        second(a)
    scale = 1.0 / (count - 1.0)
    sent = []

    def place(j, n, src, dst_rows, delta, block, mirrored):
        row_panel = lax.rem(c + delta, NC)
        target = row_panel * 4 + block
        dst = land.at[j, dst_rows]
        here = make_local(src, dst, fin_r.at[j])
        there = remote(src, dst, fin_s.at[j, n], fin_r.at[j], (target, c))
        same = target == f

        @pl.when(same)
        def _():
            here.start()

        @pl.when(jnp.logical_not(same))
        def _():
            there.start()

        sent.append((jnp.logical_not(same), there))
        turned = remote(src, land.at[block, dst_rows], fin_s.at[j, n + 3], fin_r.at[block], (c * 4 + j, row_panel))

        @pl.when(mirrored)
        def _():
            turned.start()

        sent.append((mirrored, turned))

    def make_local(src, dst, sem):
        return pltpu.make_async_copy(src, dst, sem)

    def deliver(j, total):
        fr[j] = (total * scale).reshape(UNIT // 8, 8, LANES)
        for p in range(2):
            place(j, p, fr.at[j, pl.ds(4 * p, 4)], pl.ds(4 * yy, 4), zz // 2, lax.rem(zz, 2) * 2 + p, zz >= 2)
        e = zz // 4
        place(j, 2, fr.at[j, pl.ds(8, 1)], pl.ds(4 * yy + lax.rem(zz, 4), 1), 4, far_block(j, e), zz >= 0)

    total = rb[yy].astype(F32)
    for o in range(1, NY):
        by_copies[o - 1].wait_recv()
        total = total + by[o - 1].astype(F32)
    deliver(NA, total)
    for a in range(NA):
        total = ra[a, zz].astype(F32)
        for o in range(1, NZ):
            az_copies[a][o - 1].wait_recv()
            total = total + az[a, o - 1].astype(F32)
        deliver(a, total)

    delta = lax.rem(f // 4 - c + NC, NC)
    for j in range(NA + 1):
        remote(land.at[j], land.at[j], fin_s.at[j, 0], fin_r.at[j], sib).wait_recv()
        block = land[j].reshape(OWN, LANES)
        off = lax.rem(j - lax.rem(f, 4) + 4, 4) - c // 4
        straight = jnp.where(delta == 4, jnp.logical_and(off >= 0, off <= 1), delta < 4)
        cov_ref[:, j * LANES : (j + 1) * LANES] = jnp.where(straight, block, block.T)
    for going, cp in sent:

        @pl.when(going)
        def _(cp=cp):
            cp.wait_send()

    for ring in (*ring_a, ring_b):
        ring.drain()
    for copies in (*az_copies, by_copies, xz_copies, xy_copies, sz_copies, sy_copies, col_copies):
        for cp in copies:
            cp.wait_send()
    for cp in (v_up, v_dn, v_dn_rest, v_sib, f_up, f_dn, s_up):
        cp.wait_send()

    @pl.when(kk == 0)
    def _():
        s_op.wait_send()


def on_device(frames, b_values, b_cols, frame_window):
    rows, cart = frames.shape
    vmem = pl.BlockSpec(memory_space=pltpu.VMEM)
    hbm = pl.BlockSpec(memory_space=pl.ANY)
    wrow = frame_window.reshape(1, rows)
    dma = pltpu.SemaphoreType.DMA
    count, mean, cov = pl.pallas_call(
        main_kernel,
        out_shape=(
            jax.ShapeDtypeStruct((1, 128), F32),
            jax.ShapeDtypeStruct((1, PANEL), F32),
            jax.ShapeDtypeStruct((OWN, PANEL), F32),
        ),
        in_specs=[hbm, vmem, vmem, vmem],
        out_specs=(vmem, vmem, vmem),
        scratch_shapes=[
            pltpu.VMEM((rows, cart), BF),
            pltpu.VMEM((9, BLOCK, PANEL), BF),
            pltpu.VMEM((8, 128), jnp.int32),
            pltpu.SMEM((8, 128), jnp.int32),
            pltpu.VMEM((cart // BLOCK, BLOCK, PANEL), BF),
            pltpu.VMEM((rows, PANEL), BF),
            pltpu.VMEM((cart // BLOCK, BLOCK, PANEL), BF),
            pltpu.VMEM((NC, 8, BLOCK, PANEL), BF),
            pltpu.VMEM((NC, 8, 128), jnp.int32),
            pltpu.SMEM((NC, 8, 128), jnp.int32),
            pltpu.VMEM((8, ROW), F32),
            pltpu.VMEM((NZ, 8, ROW), BF),
            pltpu.VMEM((NY, 8, ROW), BF),
            pltpu.VMEM((NZ, 1, PANEL + 128), F32),
            pltpu.VMEM((NY, 1, PANEL + 128), F32),
            pltpu.VMEM((1, cart), F32),
            pltpu.VMEM((NA, NY, NZ, UNIT, LANES), BF),
            pltpu.VMEM((NZ, NY, UNIT, LANES), BF),
            pltpu.VMEM((NA, NZ, UNIT, LANES), BF),
            pltpu.VMEM((NY, UNIT, LANES), BF),
            pltpu.VMEM((NA, 2, NY // 2, NZ, UNIT, LANES), BF),
            pltpu.VMEM((NA, NZ - 1, UNIT, LANES), BF),
            pltpu.VMEM((2, NZ // 2, NY, UNIT, LANES), BF),
            pltpu.VMEM((NY - 1, UNIT, LANES), BF),
            pltpu.VMEM((NA + 1, UNIT // 8, 8, LANES), F32),
            pltpu.VMEM((NA + 1, OWN // 8, 8, LANES), F32),
            dma((4,)), dma((3,)), dma((8,)), dma((8,)), dma((7,)), dma((7,)),
            dma((NZ - 1,)), dma((NZ - 1,)), dma((NY - 1,)), dma((NY - 1,)),
            dma((NZ - 1,)), dma((NZ - 1,)), dma((NY - 1,)), dma((NY - 1,)),
            dma((NA, 2, NY // 2)), dma((NA, 2, NY // 2)), dma((NA, NZ - 1)), dma((NA, NZ - 1)),
            dma((2, NZ // 2)), dma((2, NZ // 2)), dma((NY - 1,)), dma((NY - 1,)),
            dma((NA + 1, 6)), dma((NA + 1,)),
        ],
        compiler_params=pltpu.CompilerParams(
            collective_id=0, has_side_effects=True, vmem_limit_bytes=60 * 1024 * 1024
        ),
        name="covariance",
    )(frames, b_values.reshape(8, BLOCK, PANEL), b_cols, wrow)
    return count[0, 0], mean.reshape(PANEL), cov


def solution(mesh):
    return jax.shard_map(
        on_device,
        mesh=mesh,
        in_specs=(P("frame", None), P("coord", None), P("coord", None), P("frame")),
        out_specs=(P(), P("coord"), P("frame", "coord")),
        check_vma=False,
    )
```

```python
import functools

import jax
import jax.numpy as jnp
from jax import lax
from jax.experimental import pallas as pl
from jax.experimental.pallas import tpu as pltpu
from jax.sharding import PartitionSpec as P

BLOCK = 64
NY, NZ, NX = 4, 8, 4
NF, NC = NY * NZ, NX * 2
PANEL = 512
OWN = 128
LANES = 128
NA = 3
UNIT = 72
ROW = 640
MESH = pl.DeviceIdType.MESH
BF = jnp.bfloat16
F32 = jnp.float32


def remote(src, dst, send_sem, recv_sem, device):
    return pltpu.make_async_remote_copy(
        src_ref=src, dst_ref=dst, send_sem=send_sem, recv_sem=recv_sem, device_id=device, device_id_type=MESH
    )


class Ring:
    def __init__(self, n, pos, peer, own, recv, send_sems, recv_sems, rows):
        self.n, self.pos, self.own, self.recv = n, pos, own, recv
        self.peer = [peer(lax.rem(pos + 1, n)), peer(lax.rem(pos + n - 1, n))]
        self.send_sems, self.recv_sems, self.rows = send_sems, recv_sems, rows
        self.half = [slice(rows // 2, rows), slice(0, rows // 2)]

    def target(self, d, s):
        steps = self.n // 2 - s
        return lax.rem(self.pos + (steps if d == 0 else self.n - steps), self.n)

    def copy(self, d, s):
        t = self.target(d, s)
        if s == 0:
            src = self.own.at[t, self.half[d]]
            dst = self.recv.at[d, 0, self.half[d]]
        else:
            src = self.recv.at[d, s - 1]
            dst = self.recv.at[d, s]
        return remote(src, dst, self.send_sems.at[d, s], self.recv_sems.at[d, s], self.peer[d])

    def start(self, d, s):
        if s > 0:
            self.copy(d, s - 1).wait_recv()
            t = self.target(d, s)
            buf = self.recv.at[d, s - 1]
            if s == 1:
                h, o = self.half[d], self.half[1 - d]
                buf[h] = (buf[h].astype(F32) + self.own[t, h].astype(F32)).astype(BF)
                buf[o] = self.own[t, o]
            else:
                buf[...] = (buf[...].astype(F32) + self.own[t].astype(F32)).astype(BF)
        self.copy(d, s).start()

    def finish(self):
        last = self.n // 2 - 1
        for d in range(2):
            self.copy(d, last).wait_recv()

    def total(self, sl=slice(None)):
        last = self.n // 2 - 1
        return (
            self.own[self.pos, sl].astype(F32) + self.recv[0, last, sl].astype(F32) + self.recv[1, last, sl].astype(F32)
        )

    def drain(self):
        for d in range(2):
            for s in range(self.n // 2):
                self.copy(d, s).wait_send()


def main_kernel(
    x_hbm, vals_ref, cols_ref, wrow_ref,
    sums_ref, cov_ref,
    x, vt, found, where_sm, bdt, q, g, ball, cbuf, csm, rows8, xz, xy, sz, sy, xm, pa, pb, ra, rb, ay, az, bz, by, fr, land,
    ld_sem, loc_sem, val_s, val_r, col_s, col_r, xz_s, xz_r, xy_s, xy_r, z_s, z_r, y_s, y_r,
    ay_s, ay_r, az_s, az_r, bz_s, bz_r, by_s, by_r, fin_s, fin_r,
):
    f, c = lax.axis_index("frame"), lax.axis_index("coord")
    yy, zz = f // NZ, lax.rem(f, NZ)
    xx, kk = c // 2, lax.rem(c, 2)
    rows_total = x.shape[0]
    XT = 4
    xr = rows_total // XT
    loads = []
    for i in range(XT):
        sl = pl.ds(i * xr, xr)
        loads.append(pltpu.make_async_copy(x_hbm.at[sl], x.at[sl], ld_sem.at[i]))
    for cp in loads:
        cp.start()

    def coord_peer(o):
        return (f, lax.rem(c + o, NC))

    def z_peer(o):
        return (yy * NZ + lax.rem(zz + o, NZ), c)

    def y_peer(o):
        return (lax.rem(yy + o, NY) * NZ + zz, c)

    x_up = (f, lax.rem(xx + 1, NX) * 2 + kk)
    x_dn = (f, lax.rem(xx + NX - 1, NX) * 2 + kk)
    sib = (f, xx * 2 + 1 - kk)

    barrier = pltpu.get_barrier_semaphore()
    peers = [coord_peer(o) for o in range(1, NC)] + [z_peer(o) for o in range(1, NZ)] + [y_peer(o) for o in range(1, NY)]
    for p in peers:
        pl.semaphore_signal(barrier, inc=1, device_id=p, device_id_type=MESH)

    lane = lax.broadcasted_iota(jnp.int32, (8, 128), 1)
    holder = jnp.full((8, 128), 8, jnp.int32)
    for k in range(8):
        holder = jnp.where(cols_ref[:, k : k + 1] == lane, k, holder)
    found[...] = holder
    to_where = pltpu.make_async_copy(found, where_sm, loc_sem.at[2])
    to_where.start()
    vt[0:8] = vals_ref[...].reshape(PANEL, PANEL).T.reshape(8, BLOCK, PANEL)
    vt[8] = jnp.zeros((BLOCK, PANEL), BF)
    to_where.wait()

    def spread(b, carry):
        for r in range(8):
            lanes = slice(r * BLOCK, (r + 1) * BLOCK)
            bdt[b, :, lanes] = vt[where_sm[r, b], :, lanes]
        return carry

    lax.fori_loop(0, bdt.shape[0], spread, 0)
    pl.semaphore_wait(barrier, len(peers))

    c_up, c_dn, c_op = x_up[1], x_dn[1], lax.rem(c + 4, NC)
    lo, hi = pl.ds(0, 3), pl.ds(3, 5)
    own_vals = pltpu.make_async_copy(vals_ref, ball.at[c], loc_sem.at[0])
    own_vals.start()
    cbuf[c, :, 0:8] = cols_ref[...]
    cbuf[c, :, 8:] = jnp.zeros((8, 120), jnp.int32)
    v_up = remote(vals_ref.at[hi], ball.at[c, hi], val_s.at[0], val_r.at[0], x_up)
    v_dn = remote(vals_ref.at[lo], ball.at[c, lo], val_s.at[1], val_r.at[1], x_dn)
    v_dn_rest = remote(vals_ref.at[hi], ball.at[c, hi], val_s.at[4], val_r.at[4], x_dn)
    v_sib = remote(vals_ref, ball.at[c], val_s.at[2], val_r.at[2], sib)
    for cp in (v_up, v_dn, v_dn_rest, v_sib):
        cp.start()
    col_copies = [
        remote(cbuf.at[c], cbuf.at[c], col_s.at[o - 1], col_r.at[o - 1], coord_peer(o)) for o in range(1, NC)
    ]
    for cp in col_copies:
        cp.start()

    wrow = jnp.broadcast_to(wrow_ref[...].astype(F32), (8, rows_total))
    whalf = wrow.astype(BF)
    sums = jnp.zeros((8, x.shape[1]), F32)

    def project(i):
        sl = slice(i * xr, (i + 1) * xr)
        q[sl] = jnp.dot(x[sl], bdt[...].reshape(x.shape[1], PANEL), preferred_element_type=F32).astype(BF)

    cart = x.shape[1]
    for i in range(XT):
        loads[i].wait()
        sl = slice(i * xr, (i + 1) * xr)
        sums = sums + jnp.dot(whalf[:, sl], x[sl], preferred_element_type=F32)
        if i < XT - 1:
            project(i)

    def all_to_all(buf, mine, peer, n, send_sems, recv_sems):
        copies = [remote(buf.at[mine], buf.at[mine], send_sems.at[o - 1], recv_sems.at[o - 1], peer(o)) for o in range(1, n)]
        for cp in copies:
            cp.start()
        return copies

    def gathered(buf, copies):
        for cp in copies:
            cp.wait_recv()
        part = buf[0].astype(F32)
        for j in range(1, buf.shape[0]):
            part = part + buf[j].astype(F32)
        return part

    wide_sums = jnp.concatenate([sums[0:1], jnp.zeros((1, 8 * ROW - cart), F32)], axis=1)
    for i in range(8):
        rows8[i : i + 1] = wide_sums[:, i * ROW : (i + 1) * ROW]
    xz[zz] = rows8[...].astype(BF)
    xz_copies = all_to_all(xz, zz, z_peer, NZ, xz_s, xz_r)
    project(XT - 1)
    sz[zz, :, :PANEL] = jnp.dot(whalf, q[...], preferred_element_type=F32)[0:1]
    sz[zz, :, PANEL:] = jnp.broadcast_to(jnp.sum(wrow[0:1], axis=1, keepdims=True), (1, 128))
    sz_copies = all_to_all(sz, zz, z_peer, NZ, z_s, z_r)

    v_up.wait_recv()
    f_up = remote(ball.at[c_dn, hi], ball.at[c_dn, hi], val_s.at[3], val_r.at[3], x_up)
    f_up.start()
    v_dn.wait_recv()
    f_dn = remote(ball.at[c_up, lo], ball.at[c_up, lo], val_s.at[5], val_r.at[5], x_dn)
    f_dn.start()

    xy[yy] = gathered(xz, xz_copies).astype(BF)
    xy_copies = all_to_all(xy, yy, y_peer, NY, xy_s, xy_r)
    sy[yy] = gathered(sz, sz_copies)
    sy_copies = all_to_all(sy, yy, y_peer, NY, y_s, y_r)
    wcol = jnp.broadcast_to(wrow[0:1], (128, rows_total)).T
    v_dn_rest.wait_recv()
    s_up = remote(ball.at[c_up], ball.at[c_up], val_s.at[6], val_r.at[6], sib)
    s_up.start()
    whole_x = gathered(xy, xy_copies)
    whole = gathered(sy, sy_copies)
    sums_ref[...] = whole
    count = whole[:, PANEL : PANEL + 1]
    mean = whole[:, :PANEL] / count
    whole_x = whole_x * (1.0 / count)
    for i in range(8):
        width = min(ROW, cart - i * ROW)
        if width > 0:
            xm[:, i * ROW : i * ROW + width] = whole_x[i : i + 1, :width]
    wide = jnp.concatenate([wcol] * (PANEL // 128), axis=1)
    q[...] = (wide * (q[...].astype(F32) - mean)).astype(BF)

    GT = 384

    def g_tile(i, carry):
        start = pl.multiple_of(i * GT, 128)
        moved = (x[:, pl.ds(start, GT)].astype(F32) - xm[:, pl.ds(start, GT)]).astype(BF)
        tile = lax.dot_general(
            moved, q[...], (((0,), (0,)), ((), ())), preferred_element_type=F32
        ).astype(BF)
        for b in range(GT // BLOCK):
            g[i * (GT // BLOCK) + b] = tile[b * BLOCK : (b + 1) * BLOCK]
        return carry

    g_tiles = x.shape[1] // GT
    lax.fori_loop(0, g_tiles - 3, g_tile, 0)

    f_up.wait_recv()
    f_dn.wait_recv()
    s_op = remote(ball.at[c_op], ball.at[c_op], val_s.at[7], val_r.at[7], sib)

    @pl.when(kk == 0)
    def _():
        s_op.start()

    lax.fori_loop(g_tiles - 3, g_tiles, g_tile, 0)
    for cp in col_copies:
        cp.wait_recv()
    to_smem = pltpu.make_async_copy(cbuf, csm, loc_sem.at[1])
    to_smem.start()
    own_vals.wait()
    to_smem.wait()
    for cp in (v_sib, s_up):
        cp.wait_recv()

    @pl.when(kk == 1)
    def _():
        remote(ball.at[c_op - 1], ball.at[c_op - 1], val_s.at[7], val_r.at[7], sib).wait_recv()

    def p_rows(panel, row, lanes):
        picked = jnp.concatenate([g[csm[panel, row, k], :, lanes] for k in range(8)], axis=0)
        return jnp.dot(ball[panel, row], picked, preferred_element_type=F32)

    def keep(j, t, z, rows, value):
        if j < NA:
            pa[j, t, z, rows] = value.astype(BF)
        else:
            pb[z, t, rows] = value.astype(BF)

    def near_blocks(pair):
        def step(z, carry):
            panel = lax.rem(c + z // 2, NC)
            for p in range(2):
                for h in range(2):
                    row = (lax.rem(z, 2) * 2 + p) * 2 + h
                    out = p_rows(panel, row, slice(pair * 256, pair * 256 + 256))
                    for tt in range(2):
                        for jj in range(2):
                            part = out[tt * 32 : tt * 32 + 32, jj * LANES : (jj + 1) * LANES]
                            keep(pair * 2 + jj, 2 * h + tt, z, slice(p * 32, p * 32 + 32), part)
            return carry

        lax.fori_loop(0, NZ, step, 0)

    def far_block(j, e):
        return lax.rem(j + 4 - e - c // 4, 4)

    def far_blocks(j):
        for e in range(2):
            for h in range(2):
                out = p_rows(c_op, far_block(j, e) * 2 + h, slice(j * LANES, (j + 1) * LANES))
                for tt in range(2):
                    for zq in range(4):
                        part = out[tt * 32 + zq * 8 : tt * 32 + zq * 8 + 8]
                        keep(j, 2 * h + tt, 4 * e + zq, slice(64, 72), part)

    def y_at(o):
        return lax.rem(yy + o, NY)

    def z_at(o):
        return lax.rem(zz + o, NZ)

    ring_a = [
        Ring(NY, yy, lambda t: (t * NZ + zz, c), pa.at[a], ay.at[a], ay_s.at[a], ay_r.at[a], NZ) for a in range(NA)
    ]
    ring_b = Ring(NZ, zz, lambda t: (yy * NZ + t, c), pb, bz, bz_s, bz_r, NY)

    def both(ring, s):
        for d in range(2):
            ring.start(d, s)

    near_blocks(0)
    for j in range(2):
        far_blocks(j)
        both(ring_a[j], 0)
    near_blocks(1)
    far_blocks(3)
    both(ring_b, 0)
    far_blocks(2)
    both(ring_a[2], 0)
    both(ring_b, 1)
    both(ring_a[0], 1)
    both(ring_b, 2)
    both(ring_a[1], 1)
    both(ring_b, 3)
    both(ring_a[2], 1)

    az_copies, by_copies = [], []

    def second(a):
        ring_a[a].finish()
        ra[a] = ring_a[a].total().astype(BF)
        az_copies.append(
            [remote(ra.at[a, z_at(o)], az.at[a, o - 1], az_s.at[a, o - 1], az_r.at[a, o - 1], z_peer(o)) for o in range(1, NZ)]
        )
        for cp in az_copies[a]:
            cp.start()

    second(0)
    ring_b.finish()
    rb[...] = ring_b.total().astype(BF)
    for o in range(1, NY):
        by_copies.append(remote(rb.at[y_at(o)], by.at[o - 1], by_s.at[o - 1], by_r.at[o - 1], y_peer(o)))
    for cp in by_copies:
        cp.start()
    for a in range(1, NA):
        second(a)
    sent = []

    def place(j, n, src, dst_rows, delta, block, mirrored):
        row_panel = lax.rem(c + delta, NC)
        target = row_panel * 4 + block
        dst = land.at[j, dst_rows]
        here = make_local(src, dst, fin_r.at[j])
        there = remote(src, dst, fin_s.at[j, n], fin_r.at[j], (target, c))
        same = target == f

        @pl.when(same)
        def _():
            here.start()

        @pl.when(jnp.logical_not(same))
        def _():
            there.start()

        sent.append((jnp.logical_not(same), there))
        turned = remote(src, land.at[block, dst_rows], fin_s.at[j, n + 3], fin_r.at[block], (c * 4 + j, row_panel))

        @pl.when(mirrored)
        def _():
            turned.start()

        sent.append((mirrored, turned))

    def make_local(src, dst, sem):
        return pltpu.make_async_copy(src, dst, sem)

    def deliver(j, total):
        fr[j] = total.reshape(UNIT // 8, 8, LANES)
        for p in range(2):
            place(j, p, fr.at[j, pl.ds(4 * p, 4)], pl.ds(4 * yy, 4), zz // 2, lax.rem(zz, 2) * 2 + p, zz >= 2)
        e = zz // 4
        place(j, 2, fr.at[j, pl.ds(8, 1)], pl.ds(4 * yy + lax.rem(zz, 4), 1), 4, far_block(j, e), zz >= 0)

    total = rb[yy].astype(F32)
    for o in range(1, NY):
        by_copies[o - 1].wait_recv()
        total = total + by[o - 1].astype(F32)
    deliver(NA, total)
    for a in range(NA):
        total = ra[a, zz].astype(F32)
        for o in range(1, NZ):
            az_copies[a][o - 1].wait_recv()
            total = total + az[a, o - 1].astype(F32)
        deliver(a, total)

    delta = lax.rem(f // 4 - c + NC, NC)
    for j in range(NA + 1):
        remote(land.at[j], land.at[j], fin_s.at[j, 0], fin_r.at[j], sib).wait_recv()
        block = land[j].reshape(OWN, LANES)
        off = lax.rem(j - lax.rem(f, 4) + 4, 4) - c // 4
        straight = jnp.where(delta == 4, jnp.logical_and(off >= 0, off <= 1), delta < 4)
        cov_ref[:, j * LANES : (j + 1) * LANES] = jnp.where(straight, block, block.T)
    for going, cp in sent:

        @pl.when(going)
        def _(cp=cp):
            cp.wait_send()

    for ring in (*ring_a, ring_b):
        ring.drain()
    for copies in (*az_copies, by_copies, xz_copies, xy_copies, sz_copies, sy_copies, col_copies):
        for cp in copies:
            cp.wait_send()
    for cp in (v_up, v_dn, v_dn_rest, v_sib, f_up, f_dn, s_up):
        cp.wait_send()

    @pl.when(kk == 0)
    def _():
        s_op.wait_send()


def finish(sums_ref, raw_ref, count_ref, mean_ref, cov_ref):
    count = sums_ref[:, PANEL : PANEL + 1]
    count_ref[...] = sums_ref[:, PANEL:]
    mean_ref[...] = sums_ref[:, :PANEL] / count
    cov_ref[...] = raw_ref[...] * (1.0 / (count - 1.0))


def on_device(frames, b_values, b_cols, frame_window):
    rows, cart = frames.shape
    vmem = pl.BlockSpec(memory_space=pltpu.VMEM)
    hbm = pl.BlockSpec(memory_space=pl.ANY)
    wrow = frame_window.reshape(1, rows)
    dma = pltpu.SemaphoreType.DMA
    sums, raw = pl.pallas_call(
        main_kernel,
        out_shape=(
            jax.ShapeDtypeStruct((1, PANEL + 128), F32),
            jax.ShapeDtypeStruct((OWN, PANEL), F32),
        ),
        in_specs=[hbm, vmem, vmem, vmem],
        out_specs=(vmem, vmem),
        scratch_shapes=[
            pltpu.VMEM((rows, cart), BF),
            pltpu.VMEM((9, BLOCK, PANEL), BF),
            pltpu.VMEM((8, 128), jnp.int32),
            pltpu.SMEM((8, 128), jnp.int32),
            pltpu.VMEM((cart // BLOCK, BLOCK, PANEL), BF),
            pltpu.VMEM((rows, PANEL), BF),
            pltpu.VMEM((cart // BLOCK, BLOCK, PANEL), BF),
            pltpu.VMEM((NC, 8, BLOCK, PANEL), BF),
            pltpu.VMEM((NC, 8, 128), jnp.int32),
            pltpu.SMEM((NC, 8, 128), jnp.int32),
            pltpu.VMEM((8, ROW), F32),
            pltpu.VMEM((NZ, 8, ROW), BF),
            pltpu.VMEM((NY, 8, ROW), BF),
            pltpu.VMEM((NZ, 1, PANEL + 128), F32),
            pltpu.VMEM((NY, 1, PANEL + 128), F32),
            pltpu.VMEM((1, cart), F32),
            pltpu.VMEM((NA, NY, NZ, UNIT, LANES), BF),
            pltpu.VMEM((NZ, NY, UNIT, LANES), BF),
            pltpu.VMEM((NA, NZ, UNIT, LANES), BF),
            pltpu.VMEM((NY, UNIT, LANES), BF),
            pltpu.VMEM((NA, 2, NY // 2, NZ, UNIT, LANES), BF),
            pltpu.VMEM((NA, NZ - 1, UNIT, LANES), BF),
            pltpu.VMEM((2, NZ // 2, NY, UNIT, LANES), BF),
            pltpu.VMEM((NY - 1, UNIT, LANES), BF),
            pltpu.VMEM((NA + 1, UNIT // 8, 8, LANES), F32),
            pltpu.VMEM((NA + 1, OWN // 8, 8, LANES), F32),
            dma((4,)), dma((3,)), dma((8,)), dma((8,)), dma((7,)), dma((7,)),
            dma((NZ - 1,)), dma((NZ - 1,)), dma((NY - 1,)), dma((NY - 1,)),
            dma((NZ - 1,)), dma((NZ - 1,)), dma((NY - 1,)), dma((NY - 1,)),
            dma((NA, 2, NY // 2)), dma((NA, 2, NY // 2)), dma((NA, NZ - 1)), dma((NA, NZ - 1)),
            dma((2, NZ // 2)), dma((2, NZ // 2)), dma((NY - 1,)), dma((NY - 1,)),
            dma((NA + 1, 6)), dma((NA + 1,)),
        ],
        compiler_params=pltpu.CompilerParams(
            collective_id=0, has_side_effects=True, vmem_limit_bytes=60 * 1024 * 1024
        ),
        name="covariance",
    )(frames, b_values.reshape(8, BLOCK, PANEL), b_cols, wrow)
    count, mean, cov = pl.pallas_call(
        finish,
        out_shape=(
            jax.ShapeDtypeStruct((1, 128), F32),
            jax.ShapeDtypeStruct((1, PANEL), F32),
            jax.ShapeDtypeStruct((OWN, PANEL), F32),
        ),
        in_specs=[vmem, vmem],
        out_specs=(vmem, vmem, vmem),
        name="finish",
    )(sums, raw)
    return count[0, 0], mean.reshape(PANEL), cov


def solution(mesh):
    return jax.shard_map(
        on_device,
        mesh=mesh,
        in_specs=(P("frame", None), P("coord", None), P("coord", None), P("frame")),
        out_specs=(P(), P("coord"), P("frame", "coord")),
        check_vma=False,
    )
```
